32 devices in a mesh: sx: 8 (over y, x, core), sy: 4 (over z).
Axes of the slice: x: 2, y: 2, z: 4, core: 2. Of those that a mesh axis runs over, the one named last changes fastest.
Arguments:
- coeffs: float32 [2, 8, 16, 4, 128, 128], P(None, 'sx', None, 'sy'), may hold values from -6 to 6
- deform: float32 [2, 4], replicated, may hold values from -0.08 to 0.08
Outputs:
- spectrum: float32 [2, 128, 512, 128], P(None, 'sx', 'sy')
The draws below stay inside these ranges and needn't reach their ends.
All inputs are finite; a program needn't handle non-finite values.
Results may differ from the reference program's by a relative error of at most 0.0014.
Values sent between devices are 32-bit elements; how exact they have to be, the bound alone decides.
A program may use at most 64 MiB of HBM per device.

```python
import math
import jax
import jax.numpy as jnp
import numpy as np
from jax import lax

NODES = 4
MODES = 4
RHS = 8
FBX = 16
FBY = 128
SBX = 8
SBY = 4


def block_scale(own_key, shape, cuts, low, largest):
    def one(dim, shards_of):
        draws = jax.random.uniform(jax.random.fold_in(jax.random.fold_in(own_key, 6), dim), (shards_of,), jnp.float32, low / len(cuts), largest / len(cuts))
        return jnp.repeat(jnp.exp(draws), shape[dim] // shards_of).reshape((-1,) + (1,) * (len(shape) - dim - 1))

    gain = one(*cuts[0])
    for cut in cuts[1:]:
        gain = gain * one(*cut)
    return gain


def bell_draw(key, extent, width, bound, cuts=(), kind=jnp.bfloat16):
    factor_of = block_scale(key, extent, cuts, -0.22, 0.18) if cuts else 1.0
    array = jax.random.normal(key, extent, jnp.float32) * width * factor_of
    return jnp.minimum(jnp.maximum(array, -bound), bound).astype(kind)


def setup_inputs(seed: int = 0) -> dict:
    keys = jax.random.split(jax.random.key(seed), 3)
    coeffs = bell_draw(keys[0], (2, SBX, FBX, SBY, FBY, RHS * NODES * NODES), 1.0, 6.0, ((1, 8), (3, 4)), jnp.float32)
    deform = jnp.clip(jax.random.uniform(keys[1], (2, MODES), jnp.float32, -0.08, 0.08), -0.08, 0.08)
    return {"coeffs": coeffs, "deform": deform}


two_pi = 2.0 * math.pi
step_scale = math.sqrt(0.5)

def cheb_nodes(count):
    return (1.0 - np.cos(np.pi * (2.0 * np.arange(count) + 1.0) / (2.0 * count))) / 2.0

def lagrange_table(count):
    nodes = cheb_nodes(count)
    table = np.ones((count, 2, count))
    for target_row in range(count):
        for sibling in range(2):
            spots = (sibling + nodes) / 2.0
            for other_node in range(count):
                if other_node != target_row:
                    table[target_row, sibling] = table[target_row, sibling] * (spots - nodes[other_node]) / (nodes[target_row] - nodes[other_node])
    return table

def rotation(first_pos, second_pos, first_freq, second_freq, deform, scales):
    first_grid = first_pos[:, :, None, None] + jnp.zeros_like(second_pos)[None, None, :, :]
    second_grid = second_pos[None, None, :, :] + jnp.zeros_like(first_pos)[:, :, None, None]
    harmonic = jnp.arange(1, deform.shape[1] + 1).astype(jnp.float32) * math.pi
    summed = (first_grid + second_grid)[..., None] * harmonic
    differ = (first_grid - second_grid)[..., None] * harmonic
    first_warp = first_grid + lax.optimization_barrier(jnp.sum(deform[0] * jnp.sin(summed), axis=-1))
    second_warp = second_grid + lax.optimization_barrier(jnp.sum(deform[1] * jnp.sin(differ), axis=-1))
    angles = scales[0] * (first_warp[..., None, None] * first_freq[:, None]) + scales[1] * (second_warp[..., None, None] * second_freq[None, :])
    return (jnp.cos(angles), jnp.sin(angles))

def orient(own_pos, other_pos, own_centre, other_centre, along, deform, scales):
    if along == 0:
        return rotation(own_pos, other_pos, own_centre, other_centre, deform, scales)
    return rotation(other_pos, own_pos, other_centre, own_centre, deform, scales)

def advance(children, parents, along, parent_count, other_boxes, other_count, parent_freq, freq_count, other_freq, other_fcount, deform, nodes, scales):
    other_pos = (other_boxes.astype(jnp.float32)[:, None] + nodes[None, :]) / other_count
    other_centre = (other_freq.astype(jnp.float32) + 0.5) / other_fcount
    parent_pos = (parents.astype(jnp.float32)[:, None] + nodes[None, :]) / parent_count
    pattern = 'au,rkuyvfg->rkayvfg' if along == 0 else 'bv,rxukvfg->rxukbfg'
    pieces = []
    for freq_child in range(2):
        centre = ((2 * parent_freq + freq_child).astype(jnp.float32) + 0.5) / (2 * freq_count)
        total_real = None
        total_imag = None
        for member, boxes, weights in children:
            child_pos = (boxes.astype(jnp.float32)[:, None] + nodes[None, :]) / (2 * parent_count)
            cosine, sine = orient(child_pos, other_pos, centre, other_centre, along, deform, scales)
            real_part = member[0] * cosine + member[1] * sine
            imag_part = member[1] * cosine - member[0] * sine
            mixed_real = jnp.einsum(pattern, weights, real_part, precision=lax.Precision.HIGHEST)
            mixed_imag = jnp.einsum(pattern, weights, imag_part, precision=lax.Precision.HIGHEST)
            if total_real is None:
                total_real, total_imag = (mixed_real, mixed_imag)
            else:
                total_real, total_imag = (total_real + mixed_real, total_imag + mixed_imag)
        cosine, sine = orient(parent_pos, other_pos, centre, other_centre, along, deform, scales)
        out_real = (total_real * cosine - total_imag * sine) * step_scale
        out_imag = (total_imag * cosine + total_real * sine) * step_scale
        pieces.append(jnp.stack([out_real, out_imag], axis=0))
    if along == 0:
        joined = jnp.stack(pieces, axis=7)
        dims = joined.shape
        return joined.reshape(dims[:6] + (dims[6] * 2, dims[8]))
    joined = jnp.stack(pieces, axis=8)
    dims = joined.shape
    return joined.reshape(dims[:7] + (dims[7] * 2,))

def local_levels(state, x_boxes, y_boxes, x_freq, x_count, y_freq, y_count, deform, nodes, lagrange, scales):
    x_bits = x_boxes.shape[0].bit_length() - 1
    y_bits = y_boxes.shape[0].bit_length() - 1
    pair_idx = jnp.arange(2).astype(jnp.int32)
    for depth in range(max(x_bits, y_bits)):
        if depth < x_bits:
            pairs = x_boxes.shape[0] // 2
            dims = state.shape
            split = state.reshape(dims[0], dims[1], pairs, 2, dims[3], dims[4], dims[5], dims[6], dims[7])
            parent_boxes = jnp.arange(pairs).astype(jnp.int32)
            children = [(split[:, :, :, 0], 2 * parent_boxes, lagrange[:, 0]), (split[:, :, :, 1], 2 * parent_boxes + 1, lagrange[:, 1])]
            state = advance(children, parent_boxes, 0, pairs, y_boxes, y_boxes.shape[0], x_freq, x_count, y_freq, y_count, deform, nodes, scales)
            x_freq = (2 * x_freq[:, None] + pair_idx[None, :]).reshape(-1)
            x_count = 2 * x_count
            x_boxes = parent_boxes
        if depth < y_bits:
            pairs = y_boxes.shape[0] // 2
            dims = state.shape
            split = state.reshape(dims[0], dims[1], dims[2], dims[3], pairs, 2, dims[5], dims[6], dims[7])
            parent_boxes = jnp.arange(pairs).astype(jnp.int32)
            children = [(split[:, :, :, :, :, 0], 2 * parent_boxes, lagrange[:, 0]), (split[:, :, :, :, :, 1], 2 * parent_boxes + 1, lagrange[:, 1])]
            state = advance(children, parent_boxes, 1, pairs, x_boxes, x_boxes.shape[0], y_freq, y_count, x_freq, x_count, deform, nodes, scales)
            y_freq = (2 * y_freq[:, None] + pair_idx[None, :]).reshape(-1)
            y_count = 2 * y_count
            y_boxes = parent_boxes
    return state

def reference(coeffs, deform):
    node_count = NODES
    right_sides = RHS
    space_x = coeffs.shape[1]
    freq_x = coeffs.shape[2]
    space_y = coeffs.shape[3]
    freq_y = coeffs.shape[4]
    old = coeffs.reshape(2, space_x, freq_x, space_y, freq_y, right_sides, node_count, node_count)
    old = jnp.transpose(old, (0, 5, 1, 6, 3, 7, 2, 4))
    nodes = jnp.asarray(cheb_nodes(node_count), dtype=jnp.float32)
    lagrange = jnp.asarray(lagrange_table(node_count), dtype=jnp.float32)
    scales = (two_pi * float(space_x * freq_x), two_pi * float(space_y * freq_y))

    def single(column):
        state = column[:, None]
        x_boxes = jnp.arange(space_x).astype(jnp.int32)
        y_boxes = jnp.arange(space_y).astype(jnp.int32)
        x_freq = jnp.arange(freq_x).astype(jnp.int32)
        y_freq = jnp.arange(freq_y).astype(jnp.int32)
        final = local_levels(state, x_boxes, y_boxes, x_freq, freq_x, y_freq, freq_y, deform, nodes, lagrange, scales)
        return final[:, 0, 0, :, 0, :, :, :]
    result = lax.map(single, jnp.moveaxis(old, 1, 0))
    result = jnp.moveaxis(result, 0, 1)
    result = jnp.transpose(result, (0, 4, 5, 1, 2, 3))
    dims = result.shape
    return result.reshape(2, dims[1], dims[2], right_sides * node_count * node_count)
```

```python
import functools
import math

import jax
import jax.numpy as jnp
import numpy as np
from jax import lax
from jax.experimental import pallas as pl
from jax.experimental.pallas import tpu as pltpu
from jax.sharding import PartitionSpec as P

NODES = 4
RHS = 8
ROWS = 8
MESH = pl.DeviceIdType.MESH


def cheb_nodes(count):
    return (1.0 - np.cos(np.pi * (2.0 * np.arange(count) + 1.0) / (2.0 * count))) / 2.0


def lagrange_table(count):
    nodes = cheb_nodes(count)
    table = np.ones((count, 2, count))
    for row in range(count):
        for sibling in range(2):
            spots = (sibling + nodes) / 2.0
            for other in range(count):
                if other != row:
                    table[row, sibling] *= (spots - nodes[other]) / (nodes[row] - nodes[other])
    return table


def mix_matrix(along, right_sides, count):
    table = lagrange_table(count)
    blocks = []
    for sibling in range(2):
        weights = table[:, sibling].T
        eye = np.eye(count)
        inner = np.kron(weights, eye) if along == 0 else np.kron(eye, weights)
        blocks.append(np.kron(np.eye(right_sides), inner))
    return (np.concatenate(blocks, axis=0) * math.sqrt(0.5)).astype(np.float32)


TAYLOR_SIN = [((-1.0) ** k) * (2.0 * math.pi) ** (2 * k + 1) / math.factorial(2 * k + 1) for k in range(8)]
TAYLOR_COS = [((-1.0) ** k) * (2.0 * math.pi) ** (2 * k) / math.factorial(2 * k) for k in range(8)]


def horner(coefs, u):
    acc = coefs[-1] * u + coefs[-2]
    for c in coefs[-3::-1]:
        acc = acc * u + c
    return acc


def turns(t):
    half = jnp.floor(2.0 * t + 0.5)
    rest = t - 0.5 * half
    parity = half - 2.0 * jnp.floor(0.5 * half)
    sign = 1.0 - 2.0 * parity
    u = rest * rest
    return sign * horner(TAYLOR_COS, u), sign * rest * horner(TAYLOR_SIN, u)


def split_index(value, by):
    return lax.div(value, by), lax.rem(value, by)


def plan_of(space_x, space_y):
    steps = []
    sx, sy, row = space_x, space_y, 0
    while sx > 1 or sy > 1:
        if sx > 1:
            steps.append((0, sx, sy, row))
            row += max(8, sx * sy)
            sx //= 2
        if sy > 1:
            steps.append((1, sx, sy, row))
            row += max(8, sx * sy)
            sy //= 2
    return steps, row


def kernel(
    dims,
    deform_hbm,
    mix_hbm,
    coeffs_ref,
    out_ref,
    recv,
    twid,
    base1,
    base2,
    last1,
    last2,
    lhs_high,
    lhs_low,
    state,
    send_sem,
    recv_sem,
    deform_ref,
    mix_ref,
    deform_sem,
    mix_sem,
    plane_sem,
    go_sem,
):
    space_x, space_y, local_x, local_y, rows, modes = dims
    steps, _ = plan_of(space_x, space_y)
    chunks_y = local_y // rows
    chunks = local_x * chunks_y
    boxes = space_x * space_y
    gain_x, gain_y = space_x, space_y
    mx = lax.axis_index("sx")
    my = lax.axis_index("sy")
    me = mx * space_y + my

    barrier = pltpu.get_barrier_semaphore()

    half = space_y // 2
    side, inner = split_index(my, half)
    near_y = side * half
    far_y = (1 - side) * half
    low = side == 0

    def signal(sem, px, py):
        pl.semaphore_signal(sem, inc=1, device_id=(px, py), device_id_type=MESH)

    for o in range(half):
        signal(barrier, mx, far_y + lax.rem(inner + o, half))

    @pl.when(low)
    def _():
        for o in range(1, half):
            signal(barrier, mx, lax.rem(inner + o, half))
        for o in range(1, space_x):
            signal(barrier, lax.rem(mx + o, space_x), my)

    fetch_mix = pltpu.make_async_copy(mix_hbm, mix_ref, mix_sem)
    fetch_mix.start()
    fetch_deform = pltpu.make_async_copy(deform_hbm, deform_ref, deform_sem)
    fetch_deform.start()

    def piece(k, px, py):
        fx, fy = split_index(k, chunks_y)
        start = pl.multiple_of(py * local_y + fy * rows, 8)
        return coeffs_ref.at[:, 0, px * local_x + fx, 0, pl.ds(start, rows), :]

    def send(k, px, py):
        pltpu.make_async_remote_copy(
            src_ref=piece(k, px, py),
            dst_ref=recv.at[k, me],
            send_sem=send_sem.at[k],
            recv_sem=recv_sem.at[k],
            device_id=(px, py),
            device_id_type=MESH,
        ).start()

    @pl.when(low)
    def _():
        pl.semaphore_wait(barrier, space_y - 1 + space_x - 1)
        for o in range(1, space_x):
            signal(plane_sem, lax.rem(mx + o, space_x), my)

    @pl.when(jnp.logical_not(low))
    def _():
        pl.semaphore_wait(barrier, half)

    def send_line(k, _):
        for o in range(half):
            send(k, mx, far_y + lax.rem(inner + o, half))
        return 0

    lax.fori_loop(0, chunks, send_line, 0)

    @pl.when(low)
    def _():
        pl.semaphore_wait(plane_sem, space_x - 1)

    @pl.when(my == half - 1)
    def _():
        for o in range(half):
            signal(go_sem, mx, half + o)

    @pl.when(jnp.logical_not(low))
    def _():
        pl.semaphore_wait(go_sem, 1)

    def send_chunk(k, _):
        def send_far(i, _):
            oy, ox = split_index(i, space_x - 1)
            send(k, lax.rem(mx + 1 + ox, space_x), far_y + lax.rem(inner + oy, half))
            return 0

        def send_near(i, _):
            oy, ox = split_index(i, space_x)
            send(k, lax.rem(mx + 1 + ox, space_x), near_y + lax.rem(inner + 1 + oy, half))
            return 0

        lax.fori_loop(0, half * (space_x - 1), send_far, 0)
        lax.fori_loop(0, half * space_x - 1, send_near, 0)
        pltpu.make_async_copy(piece(k, mx, my), recv.at[k, me], recv_sem.at[k]).start()
        return 0

    lax.fori_loop(0, chunks, send_chunk, 0)
    fetch_deform.wait()

    lane = lax.broadcasted_iota(jnp.int32, (1, 128), 1)
    spots = [float(q) for q in cheb_nodes(NODES)]

    def node_of(index):
        node = jnp.full((1, 128), spots[0], jnp.float32)
        for t in range(1, NODES):
            node = jnp.where(index == t, spots[t], node)
        return node

    node_x = node_of(lane // NODES % NODES)
    node_y = node_of(lane % NODES)

    def warped(sx, sy, count):
        box = lax.broadcasted_iota(jnp.int32, (count, 128), 0)
        ax = (box // sy).astype(jnp.float32)
        ay = (box % sy).astype(jnp.float32)
        p1 = (ax + node_x) / sx
        p2 = (ay + node_y) / sy
        y1, y2 = 0.0, 0.0
        for m in range(modes):
            y1 = y1 + deform_ref[0, m] * turns((p1 + p2) * (0.5 * (m + 1)))[1]
            y2 = y2 + deform_ref[1, m] * turns((p1 - p2) * (0.5 * (m + 1)))[1]
        return p1 + y1, p2 + y2

    for along, sx, sy, row in steps[1:]:
        count = max(8, sx * sy)
        y1, y2 = warped(sx, sy, count)
        c, s = turns((y1 * (0.25 * sx)) if along == 0 else (y2 * (0.25 * sy)))
        twid[0, pl.ds(row, count), :] = c
        twid[1, pl.ds(row, count), :] = s

    y1, y2 = warped(space_x, space_y, boxes)
    for fx in range(local_x):
        for child in range(2):
            freq = (mx * local_x + fx).astype(jnp.float32) + (0.25 + 0.5 * child)
            c, s = turns(y1 * (freq * gain_x))
            base1[0, 2 * fx + child] = c
            base1[1, 2 * fx + child] = s
    twid[0, pl.ds(0, boxes), :] = y2

    def base_box(i, _):
        freq = lax.broadcasted_iota(jnp.int32, (local_y, 128), 0) + my * local_y
        warp = twid[0, pl.ds(i, 1), :]
        c, s = turns(warp * ((freq.astype(jnp.float32) + 0.5) * gain_y))
        base2[0, i] = c
        base2[1, i] = s
        return 0

    lax.fori_loop(0, boxes, base_box, 0)

    y1, y2 = warped(1, 1, 8)
    out_x = local_x * space_x
    freq = lax.broadcasted_iota(jnp.int32, (out_x, 128), 0) + mx * out_x
    c, s = turns(y1[0:1] * (freq.astype(jnp.float32) + 0.5))
    last1[0] = c
    last1[1] = s
    for child in range(space_y):
        freq = (lax.broadcasted_iota(jnp.int32, (local_y, 128), 0) + my * local_y) * space_y + child
        c, s = turns(y2[0:1] * (freq.astype(jnp.float32) + 0.5))
        last2[0, child] = c
        last2[1, child] = s

    fetch_mix.wait()

    def rotate_into(slot, pair, sibling, size, re0, im0, re1, im1):
        spot = (slot, pl.ds(pair * 4 * size, 4 * size), pl.ds(128 * sibling, 128))
        whole = jnp.concatenate([re0, im0, re1, im1], axis=0)
        high = whole.astype(jnp.bfloat16)
        lhs_high[spot] = high
        lhs_low[spot] = (whole - high.astype(jnp.float32)).astype(jnp.bfloat16)

    def pair_of(along, sy, a1, a2):
        if along == 0:
            return (a1 // 2) * sy + a2, a1 % 2
        return a1 * (sy // 2) + a2 // 2, a2 % 2

    def compute(k, _):
        pltpu.make_async_copy(recv.at[k], recv.at[k], recv_sem.at[k]).wait()
        fx, fy = split_index(k, chunks_y)
        fy_rows = pl.ds(pl.multiple_of(fy * rows, 8), rows)
        size = rows
        for number, (along, sx, sy, row) in enumerate(steps):
            slot = number % 2
            for a1 in range(sx):
                for a2 in range(sy):
                    box = a1 * sy + a2
                    pair, sibling = pair_of(along, sy, a1, a2)
                    if number == 0:
                        re, im = recv[k, box, 0], recv[k, box, 1]
                        c, s = base2[0, box, fy_rows, :], base2[1, box, fy_rows, :]
                        re, im = re * c + im * s, im * c - re * s
                        c, s = base1[0, 2 * fx, pl.ds(box, 1), :], base1[1, 2 * fx, pl.ds(box, 1), :]
                        re0, im0 = re * c + im * s, im * c - re * s
                        c, s = base1[0, 2 * fx + 1, pl.ds(box, 1), :], base1[1, 2 * fx + 1, pl.ds(box, 1), :]
                        re1, im1 = re * c + im * s, im * c - re * s
                    else:
                        at = box * 2 * size
                        half = size // 2
                        re = jnp.concatenate(
                            [state[pl.ds(at, half), :], state[pl.ds(at + 2 * half, half), :]], axis=0
                        )
                        im = jnp.concatenate(
                            [state[pl.ds(at + half, half), :], state[pl.ds(at + 3 * half, half), :]], axis=0
                        )
                        c, s = twid[0, pl.ds(row + box, 1), :], twid[1, pl.ds(row + box, 1), :]
                        rc, rs, ic, js = re * c, re * s, im * c, im * s
                        re0, im0 = rc - js, ic + rs
                        re1, im1 = rc + js, ic - rs
                    rotate_into(slot, pair, sibling, size, re0, im0, re1, im1)
            by_high = jnp.dot(lhs_high[slot], mix_ref[along], preferred_element_type=jnp.float32)
            by_low = jnp.dot(lhs_low[slot], mix_ref[along, :, 0:128], preferred_element_type=jnp.float32)
            state[...] = by_high[:, 0:128] + (by_high[:, 128:256] + by_low)
            size *= 2
        total = len(steps)
        for code in range(1 << total):
            bits = [(code >> n) & 1 for n in range(total)]
            at = 0
            for n in range(total - 1):
                at += bits[n] * rows * (1 << n)
            half = rows * (1 << (total - 1))
            at += bits[total - 1] * 2 * half
            bx, by = 0, 0
            for n, (along, _, _, _) in enumerate(steps):
                if along == 0:
                    bx = 2 * bx + bits[n]
                else:
                    by = 2 * by + bits[n]
            re = state[pl.ds(at, rows), :]
            im = state[pl.ds(at + half, rows), :]
            first = fx * space_x + bx
            c1, s1 = last1[0, pl.ds(first, 1), :], last1[1, pl.ds(first, 1), :]
            c2, s2 = last2[0, by, fy_rows, :], last2[1, by, fy_rows, :]
            c = c1 * c2 - s1 * s2
            s = s1 * c2 + c1 * s2
            spots = pl.ds(fy * (rows * space_y) + by, rows, stride=space_y)
            out_ref[0, first, spots, :] = re * c - im * s
            out_ref[1, first, spots, :] = im * c + re * s
        return 0

    lax.fori_loop(0, chunks, compute, 0)

    def drain(k, _):
        sent = recv.at[k, pl.ds(0, boxes - 1)]
        pltpu.make_async_copy(sent, sent, send_sem.at[k]).wait()
        return 0

    lax.fori_loop(0, chunks, drain, 0)


def body(coeffs, deform):
    space_x, space_y = lax.axis_size("sx"), lax.axis_size("sy")
    _, _, freq_x, _, freq_y, lanes = coeffs.shape
    local_x, local_y = freq_x // space_x, freq_y // space_y
    rows = ROWS
    chunks = local_x * local_y // rows
    boxes = space_x * space_y
    out_x, out_y = local_x * space_x, local_y * space_y
    right_sides = lanes // NODES**2
    mix = np.stack([mix_matrix(0, right_sides, NODES), mix_matrix(1, right_sides, NODES)])
    high = mix.astype(jnp.bfloat16)
    low = (mix - high.astype(np.float32)).astype(jnp.bfloat16)
    mix = jnp.asarray(np.concatenate([high, low], axis=2))
    _, twid_rows = plan_of(space_x, space_y)
    dims = (space_x, space_y, local_x, local_y, rows, deform.shape[1])
    vmem = pl.BlockSpec(memory_space=pltpu.VMEM)
    state_rows = boxes * 2 * rows
    f32 = jnp.float32
    return pl.pallas_call(
        functools.partial(kernel, dims),
        out_shape=pltpu.VMEM((2, out_x, out_y, lanes), f32),
        in_specs=[
            pl.BlockSpec(memory_space=pl.ANY),
            pl.BlockSpec(memory_space=pl.ANY),
            pl.BlockSpec(memory_space=pl.ANY),
        ],
        out_specs=vmem,
        scratch_shapes=[
            pltpu.VMEM((chunks, boxes, 2, rows, lanes), f32),
            pltpu.VMEM((2, twid_rows, lanes), f32),
            pltpu.VMEM((2, 2 * local_x, boxes, lanes), f32),
            pltpu.VMEM((2, boxes, local_y, lanes), f32),
            pltpu.VMEM((2, out_x, lanes), f32),
            pltpu.VMEM((2, space_y, local_y, lanes), f32),
            pltpu.VMEM((2, state_rows, 2 * lanes), jnp.bfloat16),
            pltpu.VMEM((2, state_rows, 2 * lanes), jnp.bfloat16),
            pltpu.VMEM((state_rows, lanes), f32),
            pltpu.SemaphoreType.DMA((chunks,)),
            pltpu.SemaphoreType.DMA((chunks,)),
            pltpu.SMEM(deform.shape, f32),
            pltpu.VMEM(mix.shape, mix.dtype),
            pltpu.SemaphoreType.DMA,
            pltpu.SemaphoreType.DMA,
            pltpu.SemaphoreType.REGULAR,
            pltpu.SemaphoreType.REGULAR,
        ],
        compiler_params=pltpu.CompilerParams(collective_id=0, has_side_effects=True),
        name="butterfly",
    )(deform, mix, coeffs)


def solution(mesh):
    placed = (P(None, "sx", None, "sy", None, None), P())
    return jax.shard_map(
        body, mesh=mesh, in_specs=placed, out_specs=P(None, "sx", "sy", None), check_vma=False
    )
```

```python
import functools
import math

import jax
import jax.numpy as jnp
import numpy as np
from jax import lax
from jax.experimental import pallas as pl
from jax.experimental.pallas import tpu as pltpu
from jax.sharding import PartitionSpec as P

NODES = 4
FIRST = 2
VMEM_ROOM = 67043328
RHS = 8
ROWS = 8
MESH = pl.DeviceIdType.MESH


def cheb_nodes(count):
    return (1.0 - np.cos(np.pi * (2.0 * np.arange(count) + 1.0) / (2.0 * count))) / 2.0


def lagrange_table(count):
    nodes = cheb_nodes(count)
    table = np.ones((count, 2, count))
    for row in range(count):
        for sibling in range(2):
            spots = (sibling + nodes) / 2.0
            for other in range(count):
                if other != row:
                    table[row, sibling] *= (spots - nodes[other]) / (nodes[row] - nodes[other])
    return table


def mix_matrix(along, right_sides, count):
    table = lagrange_table(count)
    blocks = []
    for sibling in range(2):
        weights = table[:, sibling].T
        eye = np.eye(count)
        inner = np.kron(weights, eye) if along == 0 else np.kron(eye, weights)
        blocks.append(np.kron(np.eye(right_sides), inner))
    return (np.concatenate(blocks, axis=0) * math.sqrt(0.5)).astype(np.float32)


TAYLOR_SIN = [((-1.0) ** k) * (2.0 * math.pi) ** (2 * k + 1) / math.factorial(2 * k + 1) for k in range(8)]
TAYLOR_COS = [((-1.0) ** k) * (2.0 * math.pi) ** (2 * k) / math.factorial(2 * k) for k in range(8)]


def horner(coefs, u):
    acc = coefs[-1] * u + coefs[-2]
    for c in coefs[-3::-1]:
        acc = acc * u + c
    return acc


def turns(t):
    half = jnp.floor(2.0 * t + 0.5)
    rest = t - 0.5 * half
    parity = half - 2.0 * jnp.floor(0.5 * half)
    sign = 1.0 - 2.0 * parity
    u = rest * rest
    return sign * horner(TAYLOR_COS, u), sign * rest * horner(TAYLOR_SIN, u)


def split_index(value, by):
    return lax.div(value, by), lax.rem(value, by)


def plan_of(space_x, space_y):
    steps = []
    sx, sy, row = space_x, space_y, 0
    while sx > 1 or sy > 1:
        if sx > 1:
            steps.append((0, sx, sy, row))
            row += max(8, sx * sy)
            sx //= 2
        if sy > 1:
            steps.append((1, sx, sy, row))
            row += max(8, sx * sy)
            sy //= 2
    return steps, row


def butterfly_steps(dims, refs):
    space_x, space_y, local_x, local_y, rows, _ = dims
    recv, twid, base1, base2, last1, last2, mix_ref, lhs_high, lhs_low, state = refs
    steps, _ = plan_of(space_x, space_y)
    split = max(n for n, step in enumerate(steps) if step[0] == 1)
    chunks_y = local_y // rows
    state_rows = space_x * space_y * 2 * rows

    def place(k):
        fx, fy = split_index(k, chunks_y)
        return fx, fy, pl.ds(pl.multiple_of(fy * rows, 8), rows)

    def rotate_into(slot, pair, sibling, size, re0, im0, re1, im1):
        spot = (slot, pl.ds(pair * 4 * size, 4 * size), pl.ds(128 * sibling, 128))
        whole = jnp.concatenate([re0, im0, re1, im1], axis=0)
        high = whole.astype(jnp.bfloat16)
        lhs_high[spot] = high
        lhs_low[spot] = (whole - high.astype(jnp.float32)).astype(jnp.bfloat16)

    def rotate(number, k, first_y, count_y):
        along, sx, sy, row = steps[number]
        fx, _, fy_rows = place(k)
        size = rows << number
        for a1 in range(sx):
            for j in range(count_y):
                table = a1 * sy + first_y + j
                if along == 0:
                    pair, sibling = (a1 // 2) * count_y + j, a1 % 2
                else:
                    pair, sibling = a1 * (count_y + 1 >> 1) + j // 2, j % 2
                if number == 0:
                    re, im = recv[k, table, 0], recv[k, table, 1]
                    c, s = base2[0, table, fy_rows, :], base2[1, table, fy_rows, :]
                    re, im = re * c + im * s, im * c - re * s
                    spot = pl.ds(table, 1)
                    c, s = base1[0, 2 * fx, spot, :], base1[1, 2 * fx, spot, :]
                    re0, im0 = re * c + im * s, im * c - re * s
                    c, s = base1[0, 2 * fx + 1, spot, :], base1[1, 2 * fx + 1, spot, :]
                    re1, im1 = re * c + im * s, im * c - re * s
                else:
                    at = (a1 * count_y + j) * 2 * size
                    half = size // 2
                    re = jnp.concatenate(
                        [state[pl.ds(at, half), :], state[pl.ds(at + 2 * half, half), :]], axis=0
                    )
                    im = jnp.concatenate(
                        [state[pl.ds(at + half, half), :], state[pl.ds(at + 3 * half, half), :]], axis=0
                    )
                    spot = pl.ds(row + table, 1)
                    c, s = twid[0, spot, :], twid[1, spot, :]
                    rc, rs, ic, js = re * c, re * s, im * c, im * s
                    re0, im0 = rc - js, ic + rs
                    re1, im1 = rc + js, ic - rs
                rotate_into(number % 2, pair, sibling, size, re0, im0, re1, im1)

    def mixed(number, count):
        slot, along = number % 2, steps[number][0]
        by_high = jnp.dot(
            lhs_high[slot, 0:count], mix_ref[along], preferred_element_type=jnp.float32
        )
        by_low = jnp.dot(
            lhs_low[slot, 0:count], mix_ref[along, :, 0:128], preferred_element_type=jnp.float32
        )
        return by_high[:, 0:128] + (by_high[:, 128:256] + by_low)

    def mixed_half(number, side):
        slot, along = number % 2, steps[number][0]
        deep = pl.ds(pl.multiple_of(side * 128, 128), 128)
        by_high = jnp.dot(
            lhs_high[slot, :, 0:128], mix_ref[along, deep, :], preferred_element_type=jnp.float32
        )
        by_low = jnp.dot(
            lhs_low[slot, :, 0:128], mix_ref[along, deep, 0:128], preferred_element_type=jnp.float32
        )
        return by_high[:, 0:128] + (by_high[:, 128:256] + by_low)

    def whole_step(number, k):
        rotate(number, k, 0, steps[number][2])
        state[...] = mixed(number, state_rows)

    def half_steps(k, side):
        for number in range(split):
            count_y = steps[number][2] // 2
            rotate(number, k, side * count_y, count_y)
            state[0 : state_rows // 2] = mixed(number, state_rows // 2)
        rotate(split, k, side, 1)
        return mixed_half(split, side)

    def finish(k, store):
        fx, fy, fy_rows = place(k)
        total = len(steps)
        ends = []
        for code in range(1 << total):
            bits = [(code >> n) & 1 for n in range(total)]
            at = 0
            for n in range(total - 1):
                at += bits[n] * rows * (1 << n)
            half = rows * (1 << (total - 1))
            at += bits[total - 1] * 2 * half
            bx, by = 0, 0
            for n, (along, _, _, _) in enumerate(steps):
                if along == 0:
                    bx = 2 * bx + bits[n]
                else:
                    by = 2 * by + bits[n]
            ends.append((bx, by, at, at + half))
        for bx, by, at_re, at_im in sorted(ends):
            re = state[pl.ds(at_re, rows), :]
            im = state[pl.ds(at_im, rows), :]
            first = fx * space_x + bx
            c1, s1 = last1[0, pl.ds(first, 1), :], last1[1, pl.ds(first, 1), :]
            c2, s2 = last2[0, by, fy_rows, :], last2[1, by, fy_rows, :]
            c = c1 * c2 - s1 * s2
            s = s1 * c2 + c1 * s2
            store(fx, fy, bx, by, re * c - im * s, im * c + re * s)

    return len(steps), split, whole_step, half_steps, finish


def kernel(
    dims,
    deform_hbm,
    mix_hbm,
    coeffs_ref,
    out_ref,
    recv,
    twid,
    base1,
    base2,
    last1,
    last2,
    mix_ref,
    near_ref,
    lhs_high,
    lhs_low,
    state,
    send_sem,
    recv_sem,
    deform_ref,
    deform_sem,
    mix_sem,
    plane_sem,
    go_sem,
    line_sem,
):
    space_x, space_y, local_x, local_y, rows, modes = dims
    steps, _ = plan_of(space_x, space_y)
    chunks_y = local_y // rows
    chunks = local_x * chunks_y
    boxes = space_x * space_y
    gain_x, gain_y = space_x, space_y
    mx = lax.axis_index("sx")
    my = lax.axis_index("sy")
    me = mx * space_y + my

    barrier = pltpu.get_barrier_semaphore()

    half = space_y // 2
    side, inner = split_index(my, half)
    near_y = side * half
    far_y = (1 - side) * half
    mirror = space_y - 1 - my
    hub = my == 0
    low = jnp.logical_and(side == 0, my > 0)
    high = side == 1

    def signal(sem, px, py):
        pl.semaphore_signal(sem, inc=1, device_id=(px, py), device_id_type=MESH)

    @pl.when(side == 0)
    def _():
        for o in range(half):
            signal(barrier, mx, half + lax.rem(inner + o, half))

    @pl.when(low)
    def _():
        signal(barrier, mx, 0)

    @pl.when(high)
    def _():
        signal(barrier, mx, mirror)

        @pl.when(mirror > 0)
        def _():
            signal(barrier, mx, 0)

    @pl.when(hub)
    def _():
        for o in range(1, space_x):
            signal(barrier, lax.rem(mx + o, space_x), 0)

    fetch_mix = pltpu.make_async_copy(mix_hbm, mix_ref, mix_sem)
    fetch_mix.start()
    fetch_deform = pltpu.make_async_copy(deform_hbm, deform_ref, deform_sem)
    fetch_deform.start()

    def piece(k, px, py):
        fx, fy = split_index(k, chunks_y)
        start = pl.multiple_of(py * local_y + fy * rows, 8)
        return coeffs_ref.at[:, 0, px * local_x + fx, 0, pl.ds(start, rows), :]

    def send(k, px, py, lane_sem=None):
        pltpu.make_async_remote_copy(
            src_ref=piece(k, px, py),
            dst_ref=recv.at[k, me],
            send_sem=send_sem.at[k],
            recv_sem=recv_sem.at[k if lane_sem is None else lane_sem],
            device_id=(px, py),
            device_id_type=MESH,
        ).start()

    def send_across(k, px, py):
        send(k, px, py, jnp.where(k == chunks - 1, chunks, k))

    def send_line(py):
        def send_one(k, _):
            send_across(k, mx, py)
            return 0

        lax.fori_loop(0, chunks, send_one, 0)

    @pl.when(hub)
    def _():
        pl.semaphore_wait(barrier, space_y - 1 + space_x - 1)
        for o in range(1, space_x):
            signal(plane_sem, lax.rem(mx + o, space_x), 0)
        for o in range(half):
            send_line(half + o)
        pl.semaphore_wait(plane_sem, space_x - 1)
        for o in range(1, space_y):
            signal(go_sem, mx, o)

    @pl.when(low)
    def _():
        pl.semaphore_wait(barrier, 1)
        send_line(mirror)
        pl.semaphore_wait(line_sem, half - 1)
        for o in range(1, half):
            send_line(half + lax.rem(mirror - half + o, half))
        pl.semaphore_wait(go_sem, 1)

    @pl.when(high)
    def _():
        pl.semaphore_wait(barrier, half)
        for o in range(1, half):

            @pl.when(o != mirror)
            def _():
                signal(line_sem, mx, o)

        for o in range(half):
            send_line(half - 1 - o)
        pl.semaphore_wait(go_sem, 1)

    def ahead(px, py):
        return jnp.logical_and(px < FIRST, py == 0)

    for c in range(FIRST):

        @pl.when(jnp.logical_and(jnp.logical_or(mx != c, low), me != c * space_y))
        def _():
            send(0, c, 0)

    def send_chunk(k, _):
        def send_next(send_one, px, py):
            piece_k = k + ahead(px, py).astype(jnp.int32)

            @pl.when(piece_k < chunks)
            def _():
                send_one(piece_k, px, py)

        def send_far(i, _):
            oy, ox = split_index(i, space_x - 1)
            send_next(send_across, lax.rem(mx + 1 + ox, space_x), far_y + lax.rem(inner + oy, half))
            return 0

        def send_near(i, _):
            oy, ox = split_index(i, space_x)
            send_next(send, lax.rem(mx + 1 + ox, space_x), near_y + lax.rem(inner + 1 + oy, half))
            return 0

        lax.fori_loop(0, half * (space_x - 1), send_far, 0)
        lax.fori_loop(0, half * space_x - 1, send_near, 0)
        pltpu.make_async_copy(piece(k, mx, my), recv.at[k, me], recv_sem.at[k]).start()
        return 0

    lax.fori_loop(0, chunks, send_chunk, 0)
    fetch_deform.wait()

    lane = lax.broadcasted_iota(jnp.int32, (1, 128), 1)
    spots = [float(q) for q in cheb_nodes(NODES)]

    def node_of(index):
        node = jnp.full((1, 128), spots[0], jnp.float32)
        for t in range(1, NODES):
            node = jnp.where(index == t, spots[t], node)
        return node

    node_x = node_of(lane // NODES % NODES)
    node_y = node_of(lane % NODES)

    def warped(sx, sy, count):
        box = lax.broadcasted_iota(jnp.int32, (count, 128), 0)
        ax = (box // sy).astype(jnp.float32)
        ay = (box % sy).astype(jnp.float32)
        p1 = (ax + node_x) / sx
        p2 = (ay + node_y) / sy
        y1, y2 = 0.0, 0.0
        for m in range(modes):
            y1 = y1 + deform_ref[0, m] * turns((p1 + p2) * (0.5 * (m + 1)))[1]
            y2 = y2 + deform_ref[1, m] * turns((p1 - p2) * (0.5 * (m + 1)))[1]
        return p1 + y1, p2 + y2

    for along, sx, sy, row in steps[1:]:
        count = max(8, sx * sy)
        y1, y2 = warped(sx, sy, count)
        c, s = turns((y1 * (0.25 * sx)) if along == 0 else (y2 * (0.25 * sy)))
        twid[0, pl.ds(row, count), :] = c
        twid[1, pl.ds(row, count), :] = s

    y1, y2 = warped(space_x, space_y, boxes)
    for fx in range(local_x):
        for child in range(2):
            freq = (mx * local_x + fx).astype(jnp.float32) + (0.25 + 0.5 * child)
            c, s = turns(y1 * (freq * gain_x))
            base1[0, 2 * fx + child] = c
            base1[1, 2 * fx + child] = s
    twid[0, pl.ds(0, boxes), :] = y2

    def base_box(i, _):
        freq = lax.broadcasted_iota(jnp.int32, (local_y, 128), 0) + my * local_y
        warp = twid[0, pl.ds(i, 1), :]
        c, s = turns(warp * ((freq.astype(jnp.float32) + 0.5) * gain_y))
        base2[0, i] = c
        base2[1, i] = s
        return 0

    lax.fori_loop(0, boxes, base_box, 0)

    y1, y2 = warped(1, 1, 8)
    out_x = local_x * space_x
    freq = lax.broadcasted_iota(jnp.int32, (out_x, 128), 0) + mx * out_x
    c, s = turns(y1[0:1] * (freq.astype(jnp.float32) + 0.5))
    last1[0] = c
    last1[1] = s
    for child in range(space_y):
        freq = (lax.broadcasted_iota(jnp.int32, (local_y, 128), 0) + my * local_y) * space_y + child
        c, s = turns(y2[0:1] * (freq.astype(jnp.float32) + 0.5))
        last2[0, child] = c
        last2[1, child] = s

    fetch_mix.wait()

    _, _, whole_step, half_steps, finish = butterfly_steps(
        dims, (recv, twid, base1, base2, last1, last2, mix_ref, lhs_high, lhs_low, state)
    )

    def keep(fx, fy, bx, by, re, im):
        spots = pl.ds(fy * (rows * space_y) + by, rows, stride=space_y)
        out_ref[0, fx * space_x + bx, spots, :] = re
        out_ref[1, fx * space_x + bx, spots, :] = im

    def compute(k, _):
        pltpu.make_async_copy(recv.at[k], recv.at[k], recv_sem.at[k]).wait()
        for number in range(len(steps)):
            whole_step(number, k)
        finish(k, keep)
        return 0

    lax.fori_loop(0, chunks - 1, compute, 0)
    some = recv.at[chunks - 1, pl.ds(0, boxes // 2)]
    pltpu.make_async_copy(some, some, recv_sem.at[chunks - 1]).wait()
    near_ref[...] = half_steps(chunks - 1, side)
    pltpu.make_async_copy(some, some, recv_sem.at[chunks]).wait()

    def drain(k, _):
        sent = recv.at[k, pl.ds(0, boxes - 1)]
        pltpu.make_async_copy(sent, sent, send_sem.at[k]).wait()
        return 0

    lax.fori_loop(0, chunks, drain, 0)


def tail_kernel(
    dims,
    done_ref,
    recv,
    twid,
    base1,
    base2,
    last1,
    last2,
    mix_ref,
    near_ref,
    out_hbm,
    lhs_high,
    lhs_low,
    state,
    tail,
    sem,
):
    space_x, space_y, local_x, local_y, rows, _ = dims
    chunks_y = local_y // rows
    last = local_x * chunks_y - 1
    start_x, start_y = (local_x - 1) * space_x, (chunks_y - 1) * rows * space_y
    copies = []

    def copy_out(source, target):
        copies.append(pltpu.make_async_copy(source, target, sem.at[len(copies)]))
        copies[-1].start()

    if start_x:
        spot = (slice(None), pl.ds(0, start_x))
        copy_out(done_ref.at[spot], out_hbm.at[spot])
    if start_y:
        spot = (slice(None), pl.ds(start_x, space_x), pl.ds(0, start_y))
        copy_out(done_ref.at[spot], out_hbm.at[spot])

    total, split, whole_step, half_steps, finish = butterfly_steps(
        dims, (recv, twid, base1, base2, last1, last2, mix_ref, lhs_high, lhs_low, state)
    )
    far = 1 - lax.div(lax.axis_index("sy"), space_y // 2)
    state[...] = near_ref[...] + half_steps(last, far)
    for number in range(split + 1, total):
        whole_step(number, last)

    def keep(fx, fy, bx, by, re, im):
        spots = pl.ds(by, rows, stride=space_y)
        tail[0, bx, spots, :] = re
        tail[1, bx, spots, :] = im

    finish(last, keep)
    spot = (slice(None), pl.ds(start_x, space_x), pl.ds(start_y, rows * space_y))
    copy_out(tail, out_hbm.at[spot])
    for copy in copies:
        copy.wait()


def body(coeffs, deform):
    space_x, space_y = lax.axis_size("sx"), lax.axis_size("sy")
    _, _, freq_x, _, freq_y, lanes = coeffs.shape
    local_x, local_y = freq_x // space_x, freq_y // space_y
    rows = ROWS
    chunks = local_x * local_y // rows
    boxes = space_x * space_y
    out_x, out_y = local_x * space_x, local_y * space_y
    right_sides = lanes // NODES**2
    mix = np.stack([mix_matrix(0, right_sides, NODES), mix_matrix(1, right_sides, NODES)])
    high = mix.astype(jnp.bfloat16)
    low = (mix - high.astype(np.float32)).astype(jnp.bfloat16)
    mix = jnp.asarray(np.concatenate([high, low], axis=2))
    _, twid_rows = plan_of(space_x, space_y)
    dims = (space_x, space_y, local_x, local_y, rows, deform.shape[1])
    vmem = pl.BlockSpec(memory_space=pltpu.VMEM)
    state_rows = boxes * 2 * rows
    f32 = jnp.float32
    tables = [
        pltpu.VMEM((chunks, boxes, 2, rows, lanes), f32),
        pltpu.VMEM((2, twid_rows, lanes), f32),
        pltpu.VMEM((2, 2 * local_x, boxes, lanes), f32),
        pltpu.VMEM((2, boxes, local_y, lanes), f32),
        pltpu.VMEM((2, out_x, lanes), f32),
        pltpu.VMEM((2, space_y, local_y, lanes), f32),
        pltpu.VMEM(mix.shape, mix.dtype),
        pltpu.VMEM((state_rows, lanes), f32),
    ]
    work = [
        pltpu.VMEM((2, state_rows, 2 * lanes), jnp.bfloat16),
        pltpu.VMEM((2, state_rows, 2 * lanes), jnp.bfloat16),
        pltpu.VMEM((state_rows, lanes), f32),
    ]
    results = [pltpu.VMEM((2, out_x, out_y, lanes), f32)] + tables
    held = sum(math.prod(ref.shape) * np.dtype(ref.dtype).itemsize for ref in results)
    partial_out = pl.pallas_call(
        functools.partial(kernel, dims),
        out_shape=results,
        in_specs=[pl.BlockSpec(memory_space=pltpu.HBM)] * 3,
        out_specs=[vmem] * len(results),
        scratch_shapes=work
        + [
            pltpu.SemaphoreType.DMA((chunks,)),
            pltpu.SemaphoreType.DMA((chunks + 1,)),
            pltpu.SMEM(deform.shape, f32),
            pltpu.SemaphoreType.DMA,
            pltpu.SemaphoreType.DMA,
            pltpu.SemaphoreType.REGULAR,
            pltpu.SemaphoreType.REGULAR,
            pltpu.SemaphoreType.REGULAR,
        ],
        compiler_params=pltpu.CompilerParams(
            collective_id=0, has_side_effects=True, vmem_limit_bytes=VMEM_ROOM - held - 65536
        ),
        name="butterfly",
    )(deform, mix, coeffs)
    return pl.pallas_call(
        functools.partial(tail_kernel, dims),
        out_shape=jax.ShapeDtypeStruct((2, out_x, out_y, lanes), f32),
        in_specs=[vmem] * len(results),
        out_specs=pl.BlockSpec(memory_space=pl.ANY),
        scratch_shapes=work
        + [
            pltpu.VMEM((2, space_x, rows * space_y, lanes), f32),
            pltpu.SemaphoreType.DMA((3,)),
        ],
        compiler_params=pltpu.CompilerParams(vmem_limit_bytes=VMEM_ROOM // 4),
        name="tail",
    )(*partial_out)


def solution(mesh):
    placed = (P(None, "sx", None, "sy", None, None), P())
    return jax.shard_map(
        body, mesh=mesh, in_specs=placed, out_specs=P(None, "sx", "sy", None), check_vma=False
    )
```

```python
import functools
import math

import jax
import jax.numpy as jnp
import numpy as np
from jax import lax
from jax.experimental import pallas as pl
from jax.experimental.pallas import tpu as pltpu
from jax.sharding import PartitionSpec as P

NODES = 4
FIRST = 2
VMEM_ROOM = 67043328
RHS = 8
ROWS = 8
MESH = pl.DeviceIdType.MESH


def cheb_nodes(count):
    return (1.0 - np.cos(np.pi * (2.0 * np.arange(count) + 1.0) / (2.0 * count))) / 2.0


def lagrange_table(count):
    nodes = cheb_nodes(count)
    table = np.ones((count, 2, count))
    for row in range(count):
        for sibling in range(2):
            spots = (sibling + nodes) / 2.0
            for other in range(count):
                if other != row:
                    table[row, sibling] *= (spots - nodes[other]) / (nodes[row] - nodes[other])
    return table


def mix_matrix(along, right_sides, count):
    table = lagrange_table(count)
    blocks = []
    for sibling in range(2):
        weights = table[:, sibling].T
        eye = np.eye(count)
        inner = np.kron(weights, eye) if along == 0 else np.kron(eye, weights)
        blocks.append(np.kron(np.eye(right_sides), inner))
    return (np.concatenate(blocks, axis=0) * math.sqrt(0.5)).astype(np.float32)


TAYLOR_SIN = [((-1.0) ** k) * (2.0 * math.pi) ** (2 * k + 1) / math.factorial(2 * k + 1) for k in range(8)]
TAYLOR_COS = [((-1.0) ** k) * (2.0 * math.pi) ** (2 * k) / math.factorial(2 * k) for k in range(8)]


def horner(coefs, u):
    acc = coefs[-1] * u + coefs[-2]
    for c in coefs[-3::-1]:
        acc = acc * u + c
    return acc


def turns(t):
    half = jnp.floor(2.0 * t + 0.5)
    rest = t - 0.5 * half
    parity = half - 2.0 * jnp.floor(0.5 * half)
    sign = 1.0 - 2.0 * parity
    u = rest * rest
    return sign * horner(TAYLOR_COS, u), sign * rest * horner(TAYLOR_SIN, u)


def split_index(value, by):
    return lax.div(value, by), lax.rem(value, by)


def plan_of(space_x, space_y):
    steps = []
    sx, sy, row = space_x, space_y, 0
    while sx > 1 or sy > 1:
        if sx > 1:
            steps.append((0, sx, sy, row))
            row += max(8, sx * sy)
            sx //= 2
        if sy > 1:
            steps.append((1, sx, sy, row))
            row += max(8, sx * sy)
            sy //= 2
    return steps, row


def butterfly_steps(dims, refs):
    space_x, space_y, local_x, local_y, rows, _ = dims
    recv, twid, base1, base2, last1, last2, mix_ref, lhs_high, lhs_low, state = refs
    steps, _ = plan_of(space_x, space_y)
    split = max(n for n, step in enumerate(steps) if step[0] == 1)
    chunks_y = local_y // rows
    state_rows = space_x * space_y * 2 * rows

    def place(k):
        fx, fy = split_index(k, chunks_y)
        return fx, fy, pl.ds(pl.multiple_of(fy * rows, 8), rows)

    def rotate_into(slot, pair, sibling, size, re0, im0, re1, im1):
        spot = (slot, pl.ds(pair * 4 * size, 4 * size), pl.ds(128 * sibling, 128))
        whole = jnp.concatenate([re0, im0, re1, im1], axis=0)
        high = whole.astype(jnp.bfloat16)
        lhs_high[spot] = high
        lhs_low[spot] = (whole - high.astype(jnp.float32)).astype(jnp.bfloat16)

    def rotate(number, k, first_y, count_y):
        along, sx, sy, row = steps[number]
        fx, _, fy_rows = place(k)
        size = rows << number
        for a1 in range(sx):
            for j in range(count_y):
                table = a1 * sy + first_y + j
                if along == 0:
                    pair, sibling = (a1 // 2) * count_y + j, a1 % 2
                else:
                    pair, sibling = a1 * (count_y + 1 >> 1) + j // 2, j % 2
                if number == 0:
                    re, im = recv[k, table, 0], recv[k, table, 1]
                    c, s = base2[0, table, fy_rows, :], base2[1, table, fy_rows, :]
                    re, im = re * c + im * s, im * c - re * s
                    spot = pl.ds(table, 1)
                    c, s = base1[0, 2 * fx, spot, :], base1[1, 2 * fx, spot, :]
                    re0, im0 = re * c + im * s, im * c - re * s
                    c, s = base1[0, 2 * fx + 1, spot, :], base1[1, 2 * fx + 1, spot, :]
                    re1, im1 = re * c + im * s, im * c - re * s
                else:
                    at = (a1 * count_y + j) * 2 * size
                    half = size // 2
                    re = jnp.concatenate(
                        [state[pl.ds(at, half), :], state[pl.ds(at + 2 * half, half), :]], axis=0
                    )
                    im = jnp.concatenate(
                        [state[pl.ds(at + half, half), :], state[pl.ds(at + 3 * half, half), :]], axis=0
                    )
                    spot = pl.ds(row + table, 1)
                    c, s = twid[0, spot, :], twid[1, spot, :]
                    rc, rs, ic, js = re * c, re * s, im * c, im * s
                    re0, im0 = rc - js, ic + rs
                    re1, im1 = rc + js, ic - rs
                rotate_into(number % 2, pair, sibling, size, re0, im0, re1, im1)

    def mixed(number, count):
        slot, along = number % 2, steps[number][0]
        by_high = jnp.dot(
            lhs_high[slot, 0:count], mix_ref[along], preferred_element_type=jnp.float32
        )
        by_low = jnp.dot(
            lhs_low[slot, 0:count], mix_ref[along, :, 0:128], preferred_element_type=jnp.float32
        )
        return by_high[:, 0:128] + (by_high[:, 128:256] + by_low)

    def mixed_half(number, side):
        slot, along = number % 2, steps[number][0]
        deep = pl.ds(pl.multiple_of(side * 128, 128), 128)
        by_high = jnp.dot(
            lhs_high[slot, :, 0:128], mix_ref[along, deep, :], preferred_element_type=jnp.float32
        )
        by_low = jnp.dot(
            lhs_low[slot, :, 0:128], mix_ref[along, deep, 0:128], preferred_element_type=jnp.float32
        )
        return by_high[:, 0:128] + (by_high[:, 128:256] + by_low)

    def whole_step(number, k):
        rotate(number, k, 0, steps[number][2])
        state[...] = mixed(number, state_rows)

    def half_steps(k, side):
        for number in range(split):
            count_y = steps[number][2] // 2
            rotate(number, k, side * count_y, count_y)
            state[0 : state_rows // 2] = mixed(number, state_rows // 2)
        rotate(split, k, side, 1)
        return mixed_half(split, side)

    def finish(k, store):
        fx, fy, fy_rows = place(k)
        total = len(steps)
        ends = []
        for code in range(1 << total):
            bits = [(code >> n) & 1 for n in range(total)]
            at = 0
            for n in range(total - 1):
                at += bits[n] * rows * (1 << n)
            half = rows * (1 << (total - 1))
            at += bits[total - 1] * 2 * half
            bx, by = 0, 0
            for n, (along, _, _, _) in enumerate(steps):
                if along == 0:
                    bx = 2 * bx + bits[n]
                else:
                    by = 2 * by + bits[n]
            ends.append((bx, by, at, at + half))
        for bx, by, at_re, at_im in sorted(ends):
            re = state[pl.ds(at_re, rows), :]
            im = state[pl.ds(at_im, rows), :]
            first = fx * space_x + bx
            c1, s1 = last1[0, pl.ds(first, 1), :], last1[1, pl.ds(first, 1), :]
            c2, s2 = last2[0, by, fy_rows, :], last2[1, by, fy_rows, :]
            c = c1 * c2 - s1 * s2
            s = s1 * c2 + c1 * s2
            store(fx, fy, bx, by, re * c - im * s, im * c + re * s)

    return len(steps), split, whole_step, half_steps, finish


def kernel(
    dims,
    deform_hbm,
    mix_hbm,
    coeffs_ref,
    out_ref,
    recv,
    twid,
    base1,
    base2,
    last1,
    last2,
    mix_ref,
    near_ref,
    lhs_high,
    lhs_low,
    state,
    send_sem,
    recv_sem,
    deform_ref,
    deform_sem,
    mix_sem,
    plane_sem,
    go_sem,
    line_sem,
):
    space_x, space_y, local_x, local_y, rows, modes = dims
    steps, _ = plan_of(space_x, space_y)
    chunks_y = local_y // rows
    chunks = local_x * chunks_y
    boxes = space_x * space_y
    gain_x, gain_y = space_x, space_y
    mx = lax.axis_index("sx")
    my = lax.axis_index("sy")
    me = mx * space_y + my

    barrier = pltpu.get_barrier_semaphore()

    half = space_y // 2
    side, inner = split_index(my, half)
    near_y = side * half
    far_y = (1 - side) * half
    mirror = space_y - 1 - my
    hub = my == 0
    low = jnp.logical_and(side == 0, my > 0)
    high = side == 1

    def signal(sem, px, py):
        pl.semaphore_signal(sem, inc=1, device_id=(px, py), device_id_type=MESH)

    @pl.when(side == 0)
    def _():
        for o in range(half):
            signal(barrier, mx, half + lax.rem(inner + o, half))

    @pl.when(low)
    def _():
        signal(barrier, mx, 0)

    @pl.when(high)
    def _():
        signal(barrier, mx, mirror)

        @pl.when(mirror > 0)
        def _():
            signal(barrier, mx, 0)

    @pl.when(hub)
    def _():
        for o in range(1, space_x):
            signal(barrier, lax.rem(mx + o, space_x), 0)

    fetch_mix = pltpu.make_async_copy(mix_hbm, mix_ref, mix_sem)
    fetch_mix.start()
    fetch_deform = pltpu.make_async_copy(deform_hbm, deform_ref, deform_sem)
    fetch_deform.start()

    def piece(k, px, py):
        fx, fy = split_index(k, chunks_y)
        start = pl.multiple_of(py * local_y + fy * rows, 8)
        return coeffs_ref.at[:, 0, px * local_x + fx, 0, pl.ds(start, rows), :]

    def send(k, px, py, lane_sem=None):
        pltpu.make_async_remote_copy(
            src_ref=piece(k, px, py),
            dst_ref=recv.at[k, me],
            send_sem=send_sem,
            recv_sem=recv_sem.at[k if lane_sem is None else lane_sem],
            device_id=(px, py),
            device_id_type=MESH,
        ).start()

    def send_across(k, px, py):
        send(k, px, py, jnp.where(k == chunks - 1, chunks, k))

    def send_line(py):
        def send_one(k, _):
            send_across(k, mx, py)
            return 0

        lax.fori_loop(0, chunks, send_one, 0)

    @pl.when(hub)
    def _():
        pl.semaphore_wait(barrier, space_y - 1 + space_x - 1)
        for o in range(1, space_x):
            signal(plane_sem, lax.rem(mx + o, space_x), 0)
        for o in range(half):
            send_line(half + o)
        pl.semaphore_wait(plane_sem, space_x - 1)
        for o in range(1, space_y):
            signal(go_sem, mx, o)

    @pl.when(low)
    def _():
        pl.semaphore_wait(barrier, 1)
        send_line(mirror)
        pl.semaphore_wait(line_sem, half - 1)
        for o in range(1, half):
            send_line(half + lax.rem(mirror - half + o, half))
        pl.semaphore_wait(go_sem, 1)

    @pl.when(high)
    def _():
        pl.semaphore_wait(barrier, half)
        for o in range(1, half):

            @pl.when(o != mirror)
            def _():
                signal(line_sem, mx, o)

        for o in range(half):
            send_line(half - 1 - o)
        pl.semaphore_wait(go_sem, 1)

    def ahead(px):
        return jnp.where(px < FIRST, 1, 0)

    for c in range(FIRST):
        for o in range(half):

            @pl.when(mx != c)
            def _():
                send(0, c, far_y + lax.rem(inner + o, half))

            @pl.when(jnp.logical_or(mx != c, o > 0))
            def _():
                send(0, c, near_y + lax.rem(inner + o, half))

    def send_chunk(k, _):
        def send_next(send_one, px, py):
            piece_k = k + ahead(px)

            @pl.when(piece_k < chunks)
            def _():
                send_one(piece_k, px, py)

        def send_far(i, _):
            oy, ox = split_index(i, space_x - 1)
            send_next(send_across, lax.rem(mx + 1 + ox, space_x), far_y + lax.rem(inner + oy, half))
            return 0

        def send_near(i, _):
            oy, ox = split_index(i, space_x)
            send_next(send, lax.rem(mx + 1 + ox, space_x), near_y + lax.rem(inner + 1 + oy, half))
            return 0

        lax.fori_loop(0, half * (space_x - 1), send_far, 0)
        lax.fori_loop(0, half * space_x - 1, send_near, 0)
        pltpu.make_async_copy(piece(k, mx, my), recv.at[k, me], recv_sem.at[k]).start()
        return 0

    lax.fori_loop(0, chunks, send_chunk, 0)
    fetch_deform.wait()

    lane = lax.broadcasted_iota(jnp.int32, (1, 128), 1)
    spots = [float(q) for q in cheb_nodes(NODES)]

    def node_of(index):
        node = jnp.full((1, 128), spots[0], jnp.float32)
        for t in range(1, NODES):
            node = jnp.where(index == t, spots[t], node)
        return node

    node_x = node_of(lane // NODES % NODES)
    node_y = node_of(lane % NODES)

    def warped(sx, sy, count):
        box = lax.broadcasted_iota(jnp.int32, (count, 128), 0)
        ax = (box // sy).astype(jnp.float32)
        ay = (box % sy).astype(jnp.float32)
        p1 = (ax + node_x) / sx
        p2 = (ay + node_y) / sy
        y1, y2 = 0.0, 0.0
        for m in range(modes):
            y1 = y1 + deform_ref[0, m] * turns((p1 + p2) * (0.5 * (m + 1)))[1]
            y2 = y2 + deform_ref[1, m] * turns((p1 - p2) * (0.5 * (m + 1)))[1]
        return p1 + y1, p2 + y2

    for along, sx, sy, row in steps[1:]:
        count = max(8, sx * sy)
        y1, y2 = warped(sx, sy, count)
        c, s = turns((y1 * (0.25 * sx)) if along == 0 else (y2 * (0.25 * sy)))
        twid[0, pl.ds(row, count), :] = c
        twid[1, pl.ds(row, count), :] = s

    y1, y2 = warped(space_x, space_y, boxes)
    for fx in range(local_x):
        for child in range(2):
            freq = (mx * local_x + fx).astype(jnp.float32) + (0.25 + 0.5 * child)
            c, s = turns(y1 * (freq * gain_x))
            base1[0, 2 * fx + child] = c
            base1[1, 2 * fx + child] = s
    twid[0, pl.ds(0, boxes), :] = y2

    def base_box(i, _):
        freq = lax.broadcasted_iota(jnp.int32, (local_y, 128), 0) + my * local_y
        warp = twid[0, pl.ds(i, 1), :]
        c, s = turns(warp * ((freq.astype(jnp.float32) + 0.5) * gain_y))
        base2[0, i] = c
        base2[1, i] = s
        return 0

    lax.fori_loop(0, boxes, base_box, 0)

    y1, y2 = warped(1, 1, 8)
    out_x = local_x * space_x
    freq = lax.broadcasted_iota(jnp.int32, (out_x, 128), 0) + mx * out_x
    c, s = turns(y1[0:1] * (freq.astype(jnp.float32) + 0.5))
    last1[0] = c
    last1[1] = s
    for child in range(space_y):
        freq = (lax.broadcasted_iota(jnp.int32, (local_y, 128), 0) + my * local_y) * space_y + child
        c, s = turns(y2[0:1] * (freq.astype(jnp.float32) + 0.5))
        last2[0, child] = c
        last2[1, child] = s

    fetch_mix.wait()

    _, _, whole_step, half_steps, finish = butterfly_steps(
        dims, (recv, twid, base1, base2, last1, last2, mix_ref, lhs_high, lhs_low, state)
    )

    def keep(fx, fy, bx, by, re, im):
        spots = pl.ds(fy * (rows * space_y) + by, rows, stride=space_y)
        out_ref[0, fx * space_x + bx, spots, :] = re
        out_ref[1, fx * space_x + bx, spots, :] = im

    def compute(k, _):
        pltpu.make_async_copy(recv.at[k], recv.at[k], recv_sem.at[k]).wait()
        for number in range(len(steps)):
            whole_step(number, k)
        finish(k, keep)
        return 0

    some = recv.at[chunks - 1, pl.ds(0, boxes // 2)]
    lax.fori_loop(0, chunks - 2, compute, 0)
    pltpu.make_async_copy(some, some, recv_sem.at[chunks - 1]).wait()
    near_ref[...] = half_steps(chunks - 1, side)
    lax.fori_loop(chunks - 2, chunks - 1, compute, 0)
    sent = recv.at[:, pl.ds(0, boxes - 1)]
    pltpu.make_async_copy(sent, sent, send_sem).wait()
    pltpu.make_async_copy(some, some, recv_sem.at[chunks]).wait()


def tail_kernel(
    dims,
    done_ref,
    recv,
    twid,
    base1,
    base2,
    last1,
    last2,
    mix_ref,
    near_ref,
    out_hbm,
    lhs_high,
    lhs_low,
    state,
    tail,
    sem,
):
    space_x, space_y, local_x, local_y, rows, _ = dims
    chunks_y = local_y // rows
    last = local_x * chunks_y - 1
    start_x, start_y = (local_x - 1) * space_x, (chunks_y - 1) * rows * space_y
    copies = []

    def copy_out(source, target):
        copies.append(pltpu.make_async_copy(source, target, sem.at[len(copies)]))
        copies[-1].start()

    if start_x:
        spot = (slice(None), pl.ds(0, start_x))
        copy_out(done_ref.at[spot], out_hbm.at[spot])
    if start_y:
        spot = (slice(None), pl.ds(start_x, space_x), pl.ds(0, start_y))
        copy_out(done_ref.at[spot], out_hbm.at[spot])

    total, split, whole_step, half_steps, finish = butterfly_steps(
        dims, (recv, twid, base1, base2, last1, last2, mix_ref, lhs_high, lhs_low, state)
    )
    far = 1 - lax.div(lax.axis_index("sy"), space_y // 2)
    state[...] = near_ref[...] + half_steps(last, far)
    for number in range(split + 1, total):
        whole_step(number, last)

    def keep(fx, fy, bx, by, re, im):
        spots = pl.ds(by, rows, stride=space_y)
        tail[0, bx, spots, :] = re
        tail[1, bx, spots, :] = im

    finish(last, keep)
    spot = (slice(None), pl.ds(start_x, space_x), pl.ds(start_y, rows * space_y))
    copy_out(tail, out_hbm.at[spot])
    for copy in copies:
        copy.wait()


def body(coeffs, deform):
    space_x, space_y = lax.axis_size("sx"), lax.axis_size("sy")
    _, _, freq_x, _, freq_y, lanes = coeffs.shape
    local_x, local_y = freq_x // space_x, freq_y // space_y
    rows = ROWS
    chunks = local_x * local_y // rows
    boxes = space_x * space_y
    out_x, out_y = local_x * space_x, local_y * space_y
    right_sides = lanes // NODES**2
    mix = np.stack([mix_matrix(0, right_sides, NODES), mix_matrix(1, right_sides, NODES)])
    high = mix.astype(jnp.bfloat16)
    low = (mix - high.astype(np.float32)).astype(jnp.bfloat16)
    mix = jnp.asarray(np.concatenate([high, low], axis=2))
    _, twid_rows = plan_of(space_x, space_y)
    dims = (space_x, space_y, local_x, local_y, rows, deform.shape[1])
    vmem = pl.BlockSpec(memory_space=pltpu.VMEM)
    state_rows = boxes * 2 * rows
    f32 = jnp.float32
    tables = [
        pltpu.VMEM((chunks, boxes, 2, rows, lanes), f32),
        pltpu.VMEM((2, twid_rows, lanes), f32),
        pltpu.VMEM((2, 2 * local_x, boxes, lanes), f32),
        pltpu.VMEM((2, boxes, local_y, lanes), f32),
        pltpu.VMEM((2, out_x, lanes), f32),
        pltpu.VMEM((2, space_y, local_y, lanes), f32),
        pltpu.VMEM(mix.shape, mix.dtype),
        pltpu.VMEM((state_rows, lanes), f32),
    ]
    work = [
        pltpu.VMEM((2, state_rows, 2 * lanes), jnp.bfloat16),
        pltpu.VMEM((2, state_rows, 2 * lanes), jnp.bfloat16),
        pltpu.VMEM((state_rows, lanes), f32),
    ]
    results = [pltpu.VMEM((2, out_x, out_y, lanes), f32)] + tables
    held = sum(math.prod(ref.shape) * np.dtype(ref.dtype).itemsize for ref in results)
    partial_out = pl.pallas_call(
        functools.partial(kernel, dims),
        out_shape=results,
        in_specs=[pl.BlockSpec(memory_space=pltpu.HBM)] * 3,
        out_specs=[vmem] * len(results),
        scratch_shapes=work
        + [
            pltpu.SemaphoreType.DMA,
            pltpu.SemaphoreType.DMA((chunks + 1,)),
            pltpu.SMEM(deform.shape, f32),
            pltpu.SemaphoreType.DMA,
            pltpu.SemaphoreType.DMA,
            pltpu.SemaphoreType.REGULAR,
            pltpu.SemaphoreType.REGULAR,
            pltpu.SemaphoreType.REGULAR,
        ],
        compiler_params=pltpu.CompilerParams(
            collective_id=0, has_side_effects=True, vmem_limit_bytes=VMEM_ROOM - held - 65536
        ),
        name="butterfly",
    )(deform, mix, coeffs)
    return pl.pallas_call(
        functools.partial(tail_kernel, dims),
        out_shape=jax.ShapeDtypeStruct((2, out_x, out_y, lanes), f32),
        in_specs=[vmem] * len(results),
        out_specs=pl.BlockSpec(memory_space=pl.ANY),
        scratch_shapes=work
        + [
            pltpu.VMEM((2, space_x, rows * space_y, lanes), f32),
            pltpu.SemaphoreType.DMA((3,)),
        ],
        compiler_params=pltpu.CompilerParams(vmem_limit_bytes=VMEM_ROOM // 4),
        name="tail",
    )(*partial_out)


def solution(mesh):
    placed = (P(None, "sx", None, "sy", None, None), P())
    return jax.shard_map(
        body, mesh=mesh, in_specs=placed, out_specs=P(None, "sx", "sy", None), check_vma=False
    )
```

```python
import functools
import math

import jax
import jax.numpy as jnp
import numpy as np
from jax import lax
from jax.experimental import pallas as pl
from jax.experimental.pallas import tpu as pltpu
from jax.sharding import PartitionSpec as P

NODES = 4
FIRST = 2
VMEM_ROOM = 67043328
RHS = 8
ROWS = 8
MESH = pl.DeviceIdType.MESH


def cheb_nodes(count):
    return (1.0 - np.cos(np.pi * (2.0 * np.arange(count) + 1.0) / (2.0 * count))) / 2.0


def lagrange_table(count):
    nodes = cheb_nodes(count)
    table = np.ones((count, 2, count))
    for row in range(count):
        for sibling in range(2):
            spots = (sibling + nodes) / 2.0
            for other in range(count):
                if other != row:
                    table[row, sibling] *= (spots - nodes[other]) / (nodes[row] - nodes[other])
    return table


def mix_matrix(along, right_sides, count):
    table = lagrange_table(count)
    blocks = []
    for sibling in range(2):
        weights = table[:, sibling].T
        eye = np.eye(count)
        inner = np.kron(weights, eye) if along == 0 else np.kron(eye, weights)
        blocks.append(np.kron(np.eye(right_sides), inner))
    return (np.concatenate(blocks, axis=0) * math.sqrt(0.5)).astype(np.float32)


TAYLOR_SIN = [((-1.0) ** k) * (2.0 * math.pi) ** (2 * k + 1) / math.factorial(2 * k + 1) for k in range(8)]
TAYLOR_COS = [((-1.0) ** k) * (2.0 * math.pi) ** (2 * k) / math.factorial(2 * k) for k in range(8)]


def horner(coefs, u):
    acc = coefs[-1] * u + coefs[-2]
    for c in coefs[-3::-1]:
        acc = acc * u + c
    return acc


def turns(t):
    half = jnp.floor(2.0 * t + 0.5)
    rest = t - 0.5 * half
    parity = half - 2.0 * jnp.floor(0.5 * half)
    sign = 1.0 - 2.0 * parity
    u = rest * rest
    return sign * horner(TAYLOR_COS, u), sign * rest * horner(TAYLOR_SIN, u)


def split_index(value, by):
    return lax.div(value, by), lax.rem(value, by)


def plan_of(space_x, space_y):
    steps = []
    sx, sy, row = space_x, space_y, 0
    while sx > 1 or sy > 1:
        if sx > 1:
            steps.append((0, sx, sy, row))
            row += max(8, sx * sy)
            sx //= 2
        if sy > 1:
            steps.append((1, sx, sy, row))
            row += max(8, sx * sy)
            sy //= 2
    return steps, row


def butterfly_steps(dims, refs):
    space_x, space_y, local_x, local_y, rows, _ = dims
    recv, twid, base1, base2, last1, last2, mix_ref, lhs_high, lhs_low, state = refs
    steps, _ = plan_of(space_x, space_y)
    assert all(step[0] == n % 2 for n, step in enumerate(steps)) and len(steps) % 2 == 1
    chunks_y = local_y // rows
    state_rows = space_x * space_y * 2 * rows

    def place(k):
        fx, fy = split_index(k, chunks_y)
        return fx, fy, pl.ds(pl.multiple_of(fy * rows, 8), rows)

    def rotate_into(slot, pair, sibling, size, re0, im0, re1, im1):
        lines = pl.ds(pair * 4 * size, 4 * size)
        whole = jnp.concatenate([re0, im0, re1, im1], axis=0)
        high = whole.astype(jnp.bfloat16)
        low = (whole - high.astype(jnp.float32)).astype(jnp.bfloat16)
        if sibling is None:
            lhs_high[slot, lines, 0:128] = high
            lhs_high[slot, lines, 128:256] = low
        else:
            lhs_high[slot, lines, pl.ds(128 * sibling, 128)] = high
            lhs_low[slot, lines, pl.ds(128 * sibling, 128)] = low

    def rotate(number, k, first_y, count_y, alone=False):
        along, sx, sy, row = steps[number]
        fx, _, fy_rows = place(k)
        size = rows << number
        for a1 in range(sx):
            for j in range(count_y):
                table = a1 * sy + first_y + j
                if along == 0:
                    pair, sibling = (a1 // 2) * count_y + j, a1 % 2
                else:
                    pair, sibling = a1 * (count_y + 1 >> 1) + j // 2, None if alone else j % 2
                if number == 0:
                    re, im = recv[k, table, 0], recv[k, table, 1]
                    c, s = base2[0, table, fy_rows, :], base2[1, table, fy_rows, :]
                    re, im = re * c + im * s, im * c - re * s
                    spot = pl.ds(table, 1)
                    c, s = base1[0, 2 * fx, spot, :], base1[1, 2 * fx, spot, :]
                    re0, im0 = re * c + im * s, im * c - re * s
                    c, s = base1[0, 2 * fx + 1, spot, :], base1[1, 2 * fx + 1, spot, :]
                    re1, im1 = re * c + im * s, im * c - re * s
                else:
                    at = (a1 * count_y + j) * 2 * size
                    half = size // 2
                    re = jnp.concatenate(
                        [state[pl.ds(at, half), :], state[pl.ds(at + 2 * half, half), :]], axis=0
                    )
                    im = jnp.concatenate(
                        [state[pl.ds(at + half, half), :], state[pl.ds(at + 3 * half, half), :]], axis=0
                    )
                    spot = pl.ds(row + table, 1)
                    c, s = twid[0, spot, :], twid[1, spot, :]
                    rc, rs, ic, js = re * c, re * s, im * c, im * s
                    re0, im0 = rc - js, ic + rs
                    re1, im1 = rc + js, ic - rs
                rotate_into(number % 2, pair, sibling, size, re0, im0, re1, im1)

    def mixed(number, count):
        slot, along = number % 2, steps[number][0]
        by_high = jnp.dot(
            lhs_high[slot, 0:count], mix_ref[along], preferred_element_type=jnp.float32
        )
        by_low = jnp.dot(
            lhs_low[slot, 0:count], mix_ref[along, :, 0:128], preferred_element_type=jnp.float32
        )
        return by_high[:, 0:128] + (by_high[:, 128:256] + by_low)

    def mixed_alone(number, sibling, count):
        slot, along = number % 2, steps[number][0]
        deep = mix_ref[along, pl.ds(pl.multiple_of(sibling * 128, 128), 128), :]
        both = jnp.concatenate([deep, deep], axis=0)
        by = jnp.dot(lhs_high[slot, 0:count], both, preferred_element_type=jnp.float32)
        return by[:, 0:128] + by[:, 128:256]

    def whole_step(number, k):
        rotate(number, k, 0, steps[number][2])
        state[...] = mixed(number, state_rows)

    def lone_step(number, k, line):
        box = lax.div(line, 1 << number // 2)
        sibling = lax.rem(box, 2)
        rotate(number, k, box, 1, alone=True)
        return mixed_alone(number, sibling, steps[number][1] * 4 * (rows << number))

    def subtree(k, line, level):
        for number in range(2 * level + 1):
            _, sx, _, _ = steps[number]
            count_y = (1 << level) >> (number // 2)
            first_y = lax.div(line, 1 << number // 2)
            rotate(number, k, first_y, count_y)
            count = sx * count_y * 2 * (rows << number)
            state[0:count] = mixed(number, count)
        return lone_step(2 * level + 1, k, line)

    def late_line(k, line, partials):
        for number in range(len(steps) - 1):
            _, sx, _, _ = steps[number]
            if number % 2:
                partial = partials[number // 2]
                state[0 : partial.shape[0]] = partial[...] + lone_step(number, k, line)
            else:
                rotate(number, k, lax.div(line, 1 << number // 2), 1)
                count = sx * 2 * (rows << number)
                state[0:count] = mixed(number, count)
        whole_step(len(steps) - 1, k)

    def finish(k, store):
        fx, fy, fy_rows = place(k)
        total = len(steps)
        ends = []
        for code in range(1 << total):
            bits = [(code >> n) & 1 for n in range(total)]
            at = 0
            for n in range(total - 1):
                at += bits[n] * rows * (1 << n)
            half = rows * (1 << (total - 1))
            at += bits[total - 1] * 2 * half
            bx, by = 0, 0
            for n, (along, _, _, _) in enumerate(steps):
                if along == 0:
                    bx = 2 * bx + bits[n]
                else:
                    by = 2 * by + bits[n]
            ends.append((bx, by, at, at + half))
        for bx, by, at_re, at_im in sorted(ends):
            re = state[pl.ds(at_re, rows), :]
            im = state[pl.ds(at_im, rows), :]
            first = fx * space_x + bx
            c1, s1 = last1[0, pl.ds(first, 1), :], last1[1, pl.ds(first, 1), :]
            c2, s2 = last2[0, by, fy_rows, :], last2[1, by, fy_rows, :]
            c = c1 * c2 - s1 * s2
            s = s1 * c2 + c1 * s2
            store(fx, fy, bx, by, re * c - im * s, im * c + re * s)

    return len(steps), whole_step, subtree, late_line, finish


def kernel(
    dims,
    deform_hbm,
    mix_hbm,
    coeffs_ref,
    out_ref,
    recv,
    twid,
    base1,
    base2,
    last1,
    last2,
    mix_ref,
    *refs,
):
    levels = (dims[1] - 1).bit_length()
    partials = refs[:levels]
    (
        lhs_high,
        lhs_low,
        state,
        send_sem,
        recv_sem,
        deform_ref,
        deform_sem,
        mix_sem,
        plane_sem,
        go_sem,
        line_sem,
    ) = refs[levels:]
    space_x, space_y, local_x, local_y, rows, modes = dims
    steps, _ = plan_of(space_x, space_y)
    chunks_y = local_y // rows
    chunks = local_x * chunks_y
    boxes = space_x * space_y
    gain_x, gain_y = space_x, space_y
    mx = lax.axis_index("sx")
    my = lax.axis_index("sy")
    me = mx * space_y + my

    barrier = pltpu.get_barrier_semaphore()

    half = space_y // 2
    side, inner = split_index(my, half)
    near_y = side * half
    far_y = (1 - side) * half
    mirror = space_y - 1 - my
    hub = my == 0
    at_edge = inner == (half - 1) * (1 - side)
    low = jnp.logical_and(side == 0, my > 0)
    high = side == 1

    def signal(sem, px, py):
        pl.semaphore_signal(sem, inc=1, device_id=(px, py), device_id_type=MESH)

    @pl.when(side == 0)
    def _():
        for o in range(half):
            signal(barrier, mx, half + lax.rem(inner + o, half))

    @pl.when(low)
    def _():
        signal(barrier, mx, 0)

    @pl.when(high)
    def _():
        signal(barrier, mx, mirror)

        @pl.when(mirror > 0)
        def _():
            signal(barrier, mx, 0)

    @pl.when(hub)
    def _():
        for o in range(1, space_x):
            signal(barrier, lax.rem(mx + o, space_x), 0)

    fetch_mix = pltpu.make_async_copy(mix_hbm, mix_ref, mix_sem)
    fetch_mix.start()
    fetch_deform = pltpu.make_async_copy(deform_hbm, deform_ref, deform_sem)
    fetch_deform.start()

    def piece(k, px, py):
        fx, fy = split_index(k, chunks_y)
        start = pl.multiple_of(py * local_y + fy * rows, 8)
        return coeffs_ref.at[:, 0, px * local_x + fx, 0, pl.ds(start, rows), :]

    def send(k, px, py, lane_sem=None):
        pltpu.make_async_remote_copy(
            src_ref=piece(k, px, py),
            dst_ref=recv.at[k, me],
            send_sem=send_sem,
            recv_sem=recv_sem.at[k if lane_sem is None else lane_sem],
            device_id=(px, py),
            device_id_type=MESH,
        ).start()

    def send_across(k, px, py):
        send(k, px, py, jnp.where(k == chunks - 1, jnp.where(at_edge, chunks + 1, chunks), k))

    def send_line(py):
        def send_one(k, _):
            send_across(k, mx, py)
            return 0

        lax.fori_loop(0, chunks, send_one, 0)

    @pl.when(hub)
    def _():
        pl.semaphore_wait(barrier, space_y - 1 + space_x - 1)
        for o in range(1, space_x):
            signal(plane_sem, lax.rem(mx + o, space_x), 0)
        for o in range(half):
            send_line(half + o)
        pl.semaphore_wait(plane_sem, space_x - 1)
        for o in range(1, space_y):
            signal(go_sem, mx, o)

    @pl.when(low)
    def _():
        pl.semaphore_wait(barrier, 1)
        send_line(mirror)
        pl.semaphore_wait(line_sem, half - 1)
        for o in range(1, half):
            send_line(half + lax.rem(mirror - half + o, half))
        pl.semaphore_wait(go_sem, 1)

    @pl.when(high)
    def _():
        pl.semaphore_wait(barrier, half)
        for o in range(1, half):

            @pl.when(o != mirror)
            def _():
                signal(line_sem, mx, o)

        for o in range(half):
            send_line(half - 1 - o)
        pl.semaphore_wait(go_sem, 1)

    def ahead(px):
        return jnp.where(px < FIRST, 1, 0)

    for c in range(FIRST):
        for o in range(half):

            @pl.when(mx != c)
            def _():
                send(0, c, far_y + lax.rem(inner + o, half))

            @pl.when(jnp.logical_or(mx != c, o > 0))
            def _():
                send(0, c, near_y + lax.rem(inner + o, half))

    def send_chunk(k, _):
        def send_next(send_one, px, py):
            piece_k = k + ahead(px)

            @pl.when(piece_k < chunks)
            def _():
                send_one(piece_k, px, py)

        def send_far(i, _):
            oy, ox = split_index(i, space_x - 1)
            send_next(send_across, jnp.bitwise_xor(mx, space_x - 1 - ox), far_y + lax.rem(inner + oy, half))
            return 0

        def send_near(i, _):
            oy, ox = split_index(i, space_x)
            send_next(send, lax.rem(mx + 1 + ox, space_x), near_y + lax.rem(inner + 1 + oy, half))
            return 0

        lax.fori_loop(0, half * (space_x - 1), send_far, 0)
        lax.fori_loop(0, half * space_x - 1, send_near, 0)
        pltpu.make_async_copy(piece(k, mx, my), recv.at[k, me], recv_sem.at[k]).start()
        return 0

    lax.fori_loop(0, chunks, send_chunk, 0)
    fetch_deform.wait()

    lane = lax.broadcasted_iota(jnp.int32, (1, 128), 1)
    spots = [float(q) for q in cheb_nodes(NODES)]

    def node_of(index):
        node = jnp.full((1, 128), spots[0], jnp.float32)
        for t in range(1, NODES):
            node = jnp.where(index == t, spots[t], node)
        return node

    node_x = node_of(lane // NODES % NODES)
    node_y = node_of(lane % NODES)

    def warped(sx, sy, count):
        box = lax.broadcasted_iota(jnp.int32, (count, 128), 0)
        ax = (box // sy).astype(jnp.float32)
        ay = (box % sy).astype(jnp.float32)
        p1 = (ax + node_x) / sx
        p2 = (ay + node_y) / sy
        y1, y2 = 0.0, 0.0
        for m in range(modes):
            y1 = y1 + deform_ref[0, m] * turns((p1 + p2) * (0.5 * (m + 1)))[1]
            y2 = y2 + deform_ref[1, m] * turns((p1 - p2) * (0.5 * (m + 1)))[1]
        return p1 + y1, p2 + y2

    for along, sx, sy, row in steps[1:]:
        count = max(8, sx * sy)
        y1, y2 = warped(sx, sy, count)
        c, s = turns((y1 * (0.25 * sx)) if along == 0 else (y2 * (0.25 * sy)))
        twid[0, pl.ds(row, count), :] = c
        twid[1, pl.ds(row, count), :] = s

    y1, y2 = warped(space_x, space_y, boxes)
    for fx in range(local_x):
        for child in range(2):
            freq = (mx * local_x + fx).astype(jnp.float32) + (0.25 + 0.5 * child)
            c, s = turns(y1 * (freq * gain_x))
            base1[0, 2 * fx + child] = c
            base1[1, 2 * fx + child] = s
    twid[0, pl.ds(0, boxes), :] = y2

    def base_box(i, _):
        freq = lax.broadcasted_iota(jnp.int32, (local_y, 128), 0) + my * local_y
        warp = twid[0, pl.ds(i, 1), :]
        c, s = turns(warp * ((freq.astype(jnp.float32) + 0.5) * gain_y))
        base2[0, i] = c
        base2[1, i] = s
        return 0

    lax.fori_loop(0, boxes, base_box, 0)

    y1, y2 = warped(1, 1, 8)
    out_x = local_x * space_x
    freq = lax.broadcasted_iota(jnp.int32, (out_x, 128), 0) + mx * out_x
    c, s = turns(y1[0:1] * (freq.astype(jnp.float32) + 0.5))
    last1[0] = c
    last1[1] = s
    for child in range(space_y):
        freq = (lax.broadcasted_iota(jnp.int32, (local_y, 128), 0) + my * local_y) * space_y + child
        c, s = turns(y2[0:1] * (freq.astype(jnp.float32) + 0.5))
        last2[0, child] = c
        last2[1, child] = s

    fetch_mix.wait()

    total, whole_step, subtree, _, finish = butterfly_steps(
        dims, (recv, twid, base1, base2, last1, last2, mix_ref, lhs_high, lhs_low, state)
    )

    def keep(fx, fy, bx, by, re, im):
        spots = pl.ds(fy * (rows * space_y) + by, rows, stride=space_y)
        out_ref[0, fx * space_x + bx, spots, :] = re
        out_ref[1, fx * space_x + bx, spots, :] = im

    def compute(k, _):
        pltpu.make_async_copy(recv.at[k], recv.at[k], recv_sem.at[k]).wait()
        for number in range(total):
            whole_step(number, k)
        finish(k, keep)
        return 0

    last = chunks - 1
    near = recv.at[last, pl.ds(0, boxes // 2)]
    outer = recv.at[last, pl.ds(0, (half - 1) * space_x)]
    edge = recv.at[last, pl.ds(0, space_x)]
    first, second = max(last - 2, 0), max(last - 1, 0)
    lax.fori_loop(0, first, compute, 0)
    pltpu.make_async_copy(near, near, recv_sem.at[last]).wait()
    partials[-1][...] = subtree(last, near_y, levels - 1)
    lax.fori_loop(first, second, compute, 0)
    if half > 1:
        pltpu.make_async_copy(outer, outer, recv_sem.at[chunks]).wait()
    for level in range(levels - 1):
        line = half + (1 << level) - side * (3 << level)
        partials[level][...] = subtree(last, line, level)
    lax.fori_loop(second, last, compute, 0)
    sent = recv.at[:, pl.ds(0, boxes - 1)]
    pltpu.make_async_copy(sent, sent, send_sem).wait()
    pltpu.make_async_copy(edge, edge, recv_sem.at[chunks + 1]).wait()


def tail_kernel(
    dims,
    done_ref,
    recv,
    twid,
    base1,
    base2,
    last1,
    last2,
    mix_ref,
    *refs,
):
    levels = (dims[1] - 1).bit_length()
    partials = refs[:levels]
    out_hbm, lhs_high, lhs_low, state, tail, sem = refs[levels:]
    space_x, space_y, local_x, local_y, rows, _ = dims
    chunks_y = local_y // rows
    last = local_x * chunks_y - 1
    start_x, start_y = (local_x - 1) * space_x, (chunks_y - 1) * rows * space_y
    copies = []

    def copy_out(source, target):
        copies.append(pltpu.make_async_copy(source, target, sem.at[len(copies)]))
        copies[-1].start()

    if start_x:
        spot = (slice(None), pl.ds(0, start_x))
        copy_out(done_ref.at[spot], out_hbm.at[spot])
    if start_y:
        spot = (slice(None), pl.ds(start_x, space_x), pl.ds(0, start_y))
        copy_out(done_ref.at[spot], out_hbm.at[spot])

    _, _, _, late_line, finish = butterfly_steps(
        dims, (recv, twid, base1, base2, last1, last2, mix_ref, lhs_high, lhs_low, state)
    )
    half = space_y // 2
    side = lax.div(lax.axis_index("sy"), half)
    late_line(last, half - side, partials)

    def keep(fx, fy, bx, by, re, im):
        spots = pl.ds(by, rows, stride=space_y)
        tail[0, bx, spots, :] = re
        tail[1, bx, spots, :] = im

    finish(last, keep)
    spot = (slice(None), pl.ds(start_x, space_x), pl.ds(start_y, rows * space_y))
    copy_out(tail, out_hbm.at[spot])
    for copy in copies:
        copy.wait()


def body(coeffs, deform):
    space_x, space_y = lax.axis_size("sx"), lax.axis_size("sy")
    _, _, freq_x, _, freq_y, lanes = coeffs.shape
    local_x, local_y = freq_x // space_x, freq_y // space_y
    rows = ROWS
    chunks = local_x * local_y // rows
    boxes = space_x * space_y
    out_x, out_y = local_x * space_x, local_y * space_y
    right_sides = lanes // NODES**2
    mix = np.stack([mix_matrix(0, right_sides, NODES), mix_matrix(1, right_sides, NODES)])
    high = mix.astype(jnp.bfloat16)
    low = (mix - high.astype(np.float32)).astype(jnp.bfloat16)
    mix = jnp.asarray(np.concatenate([high, low], axis=2))
    _, twid_rows = plan_of(space_x, space_y)
    dims = (space_x, space_y, local_x, local_y, rows, deform.shape[1])
    vmem = pl.BlockSpec(memory_space=pltpu.VMEM)
    state_rows = boxes * 2 * rows
    f32 = jnp.float32
    tables = [
        pltpu.VMEM((chunks, boxes, 2, rows, lanes), f32),
        pltpu.VMEM((2, twid_rows, lanes), f32),
        pltpu.VMEM((2, 2 * local_x, boxes, lanes), f32),
        pltpu.VMEM((2, boxes, local_y, lanes), f32),
        pltpu.VMEM((2, out_x, lanes), f32),
        pltpu.VMEM((2, space_y, local_y, lanes), f32),
        pltpu.VMEM(mix.shape, mix.dtype),
    ]
    tables += [
        pltpu.VMEM((sx * 4 * (rows << number), lanes), f32)
        for number, (along, sx, _, _) in enumerate(plan_of(space_x, space_y)[0])
        if along == 1
    ]
    work = [
        pltpu.VMEM((2, state_rows, 2 * lanes), jnp.bfloat16),
        pltpu.VMEM((2, state_rows, 2 * lanes), jnp.bfloat16),
        pltpu.VMEM((state_rows, lanes), f32),
    ]
    results = [pltpu.VMEM((2, out_x, out_y, lanes), f32)] + tables
    held = sum(math.prod(ref.shape) * np.dtype(ref.dtype).itemsize for ref in results)
    partial_out = pl.pallas_call(
        functools.partial(kernel, dims),
        out_shape=results,
        in_specs=[pl.BlockSpec(memory_space=pltpu.HBM)] * 3,
        out_specs=[vmem] * len(results),
        scratch_shapes=work
        + [
            pltpu.SemaphoreType.DMA,
            pltpu.SemaphoreType.DMA((chunks + 2,)),
            pltpu.SMEM(deform.shape, f32),
            pltpu.SemaphoreType.DMA,
            pltpu.SemaphoreType.DMA,
            pltpu.SemaphoreType.REGULAR,
            pltpu.SemaphoreType.REGULAR,
            pltpu.SemaphoreType.REGULAR,
        ],
        compiler_params=pltpu.CompilerParams(
            collective_id=0, has_side_effects=True, vmem_limit_bytes=VMEM_ROOM - held - 65536
        ),
        name="butterfly",
    )(deform, mix, coeffs)
    return pl.pallas_call(
        functools.partial(tail_kernel, dims),
        out_shape=jax.ShapeDtypeStruct((2, out_x, out_y, lanes), f32),
        in_specs=[vmem] * len(results),
        out_specs=pl.BlockSpec(memory_space=pl.ANY),
        scratch_shapes=work
        + [
            pltpu.VMEM((2, space_x, rows * space_y, lanes), f32),
            pltpu.SemaphoreType.DMA((3,)),
        ],
        compiler_params=pltpu.CompilerParams(vmem_limit_bytes=VMEM_ROOM // 4),
        name="tail",
    )(*partial_out)


def solution(mesh):
    placed = (P(None, "sx", None, "sy", None, None), P())
    return jax.shard_map(
        body, mesh=mesh, in_specs=placed, out_specs=P(None, "sx", "sy", None), check_vma=False
    )
```

```python
import functools
import math

import jax
import jax.numpy as jnp
import numpy as np
from jax import lax
from jax.experimental import pallas as pl
from jax.experimental.pallas import tpu as pltpu
from jax.sharding import PartitionSpec as P

NODES = 4
FIRST = 2
VMEM_ROOM = 67043328
RHS = 8
ROWS = 8
MESH = pl.DeviceIdType.MESH


def cheb_nodes(count):
    return (1.0 - np.cos(np.pi * (2.0 * np.arange(count) + 1.0) / (2.0 * count))) / 2.0


def lagrange_table(count):
    nodes = cheb_nodes(count)
    table = np.ones((count, 2, count))
    for row in range(count):
        for sibling in range(2):
            spots = (sibling + nodes) / 2.0
            for other in range(count):
                if other != row:
                    table[row, sibling] *= (spots - nodes[other]) / (nodes[row] - nodes[other])
    return table


def mix_matrix(along, right_sides, count):
    table = lagrange_table(count)
    blocks = []
    for sibling in range(2):
        weights = table[:, sibling].T
        eye = np.eye(count)
        inner = np.kron(weights, eye) if along == 0 else np.kron(eye, weights)
        blocks.append(np.kron(np.eye(right_sides), inner))
    return (np.concatenate(blocks, axis=0) * math.sqrt(0.5)).astype(np.float32)


TAYLOR_SIN = [((-1.0) ** k) * (2.0 * math.pi) ** (2 * k + 1) / math.factorial(2 * k + 1) for k in range(8)]
TAYLOR_COS = [((-1.0) ** k) * (2.0 * math.pi) ** (2 * k) / math.factorial(2 * k) for k in range(8)]


def horner(coefs, u):
    acc = coefs[-1] * u + coefs[-2]
    for c in coefs[-3::-1]:
        acc = acc * u + c
    return acc


def turns(t):
    half = jnp.floor(2.0 * t + 0.5)
    rest = t - 0.5 * half
    parity = half - 2.0 * jnp.floor(0.5 * half)
    sign = 1.0 - 2.0 * parity
    u = rest * rest
    return sign * horner(TAYLOR_COS, u), sign * rest * horner(TAYLOR_SIN, u)


def split_index(value, by):
    return lax.div(value, by), lax.rem(value, by)


def plan_of(space_x, space_y):
    steps = []
    sx, sy, row = space_x, space_y, 0
    while sx > 1 or sy > 1:
        if sx > 1:
            steps.append((0, sx, sy, row))
            row += max(8, sx * sy)
            sx //= 2
        if sy > 1:
            steps.append((1, sx, sy, row))
            row += max(8, sx * sy)
            sy //= 2
    return steps, row


def butterfly_steps(dims, refs):
    space_x, space_y, local_x, local_y, rows, _ = dims
    recv, twid, base1, base2, last1, last2, mix_ref, lhs, state = refs
    steps, _ = plan_of(space_x, space_y)
    assert all(step[0] == n % 2 for n, step in enumerate(steps)) and len(steps) % 2 == 1
    chunks_y = local_y // rows
    state_rows = space_x * space_y * 2 * rows

    def place(k):
        fx, fy = split_index(k, chunks_y)
        return fx, fy, pl.ds(pl.multiple_of(fy * rows, 8), rows)

    def rotate_into(slot, pair, sibling, size, re0, im0, re1, im1):
        lines = pl.ds(pair * 4 * size, 4 * size)
        lane = 128 * (sibling or 0)
        lhs[slot, lines, lane : lane + 128] = jnp.concatenate([re0, im0, re1, im1], axis=0)

    def parted(whole):
        high = whole.astype(jnp.bfloat16)
        return high, (whole - high.astype(jnp.float32)).astype(jnp.bfloat16)

    def rotate(number, k, first_y, count_y, alone=False):
        along, sx, sy, row = steps[number]
        fx, _, fy_rows = place(k)
        size = rows << number
        for a1 in range(sx):
            for j in range(count_y):
                table = a1 * sy + first_y + j
                if along == 0:
                    pair, sibling = (a1 // 2) * count_y + j, a1 % 2
                else:
                    pair, sibling = a1 * (count_y + 1 >> 1) + j // 2, None if alone else j % 2
                if number == 0:
                    re, im = recv[k, table, 0], recv[k, table, 1]
                    c, s = base2[0, table, fy_rows, :], base2[1, table, fy_rows, :]
                    re, im = re * c + im * s, im * c - re * s
                    spot = pl.ds(table, 1)
                    c, s = base1[0, 2 * fx, spot, :], base1[1, 2 * fx, spot, :]
                    re0, im0 = re * c + im * s, im * c - re * s
                    c, s = base1[0, 2 * fx + 1, spot, :], base1[1, 2 * fx + 1, spot, :]
                    re1, im1 = re * c + im * s, im * c - re * s
                else:
                    at = (a1 * count_y + j) * 2 * size
                    half = size // 2
                    re = jnp.concatenate(
                        [state[pl.ds(at, half), :], state[pl.ds(at + 2 * half, half), :]], axis=0
                    )
                    im = jnp.concatenate(
                        [state[pl.ds(at + half, half), :], state[pl.ds(at + 3 * half, half), :]], axis=0
                    )
                    spot = pl.ds(row + table, 1)
                    c, s = twid[0, spot, :], twid[1, spot, :]
                    rc, rs, ic, js = re * c, re * s, im * c, im * s
                    re0, im0 = rc - js, ic + rs
                    re1, im1 = rc + js, ic - rs
                rotate_into(number % 2, pair, sibling, size, re0, im0, re1, im1)

    def mixed(number, count):
        slot, along = number % 2, steps[number][0]
        high, low = parted(lhs[slot, 0:count])
        by_high = jnp.dot(high, mix_ref[along], preferred_element_type=jnp.float32)
        by_low = jnp.dot(low, mix_ref[along, :, 0:128], preferred_element_type=jnp.float32)
        return by_high[:, 0:128] + (by_high[:, 128:256] + by_low)

    def mixed_alone(number, sibling, count):
        slot, along = number % 2, steps[number][0]
        deep = mix_ref[along, pl.ds(pl.multiple_of(sibling * 128, 128), 128), :]
        both = jnp.concatenate([deep, deep], axis=0)
        pair = jnp.concatenate(parted(lhs[slot, 0:count, 0:128]), axis=1)
        by = jnp.dot(pair, both, preferred_element_type=jnp.float32)
        return by[:, 0:128] + by[:, 128:256]

    def whole_step(number, k):
        rotate(number, k, 0, steps[number][2])
        state[...] = mixed(number, state_rows)

    def lone_step(number, k, line):
        box = lax.div(line, 1 << number // 2)
        sibling = lax.rem(box, 2)
        rotate(number, k, box, 1, alone=True)
        return mixed_alone(number, sibling, steps[number][1] * 4 * (rows << number))

    def subtree(k, line, level):
        for number in range(2 * level + 1):
            _, sx, _, _ = steps[number]
            count_y = (1 << level) >> (number // 2)
            first_y = lax.div(line, 1 << number // 2)
            rotate(number, k, first_y, count_y)
            count = sx * count_y * 2 * (rows << number)
            state[0:count] = mixed(number, count)
        return lone_step(2 * level + 1, k, line)

    def late_line(k, line, partials):
        for number in range(len(steps) - 1):
            _, sx, _, _ = steps[number]
            if number % 2:
                partial = partials[number // 2]
                state[0 : partial.shape[0]] = partial[...] + lone_step(number, k, line)
            else:
                rotate(number, k, lax.div(line, 1 << number // 2), 1)
                count = sx * 2 * (rows << number)
                state[0:count] = mixed(number, count)
        whole_step(len(steps) - 1, k)

    def finish(k, store):
        fx, fy, fy_rows = place(k)
        total = len(steps)
        ends = []
        for code in range(1 << total):
            bits = [(code >> n) & 1 for n in range(total)]
            at = 0
            for n in range(total - 1):
                at += bits[n] * rows * (1 << n)
            half = rows * (1 << (total - 1))
            at += bits[total - 1] * 2 * half
            bx, by = 0, 0
            for n, (along, _, _, _) in enumerate(steps):
                if along == 0:
                    bx = 2 * bx + bits[n]
                else:
                    by = 2 * by + bits[n]
            ends.append((bx, by, at, at + half))
        for bx, by, at_re, at_im in sorted(ends):
            re = state[pl.ds(at_re, rows), :]
            im = state[pl.ds(at_im, rows), :]
            first = fx * space_x + bx
            c1, s1 = last1[0, pl.ds(first, 1), :], last1[1, pl.ds(first, 1), :]
            c2, s2 = last2[0, by, fy_rows, :], last2[1, by, fy_rows, :]
            c = c1 * c2 - s1 * s2
            s = s1 * c2 + c1 * s2
            store(fx, fy, bx, by, re * c - im * s, im * c + re * s)

    return len(steps), whole_step, subtree, late_line, finish


def kernel(
    dims,
    deform_hbm,
    mix_hbm,
    coeffs_ref,
    out_ref,
    recv,
    twid,
    base1,
    base2,
    last1,
    last2,
    mix_ref,
    *refs,
):
    levels = (dims[1] - 1).bit_length()
    partials = refs[:levels]
    (
        lhs,
        state,
        send_sem,
        recv_sem,
        deform_ref,
        deform_sem,
        mix_sem,
        plane_sem,
        go_sem,
        line_sem,
    ) = refs[levels:]
    space_x, space_y, local_x, local_y, rows, modes = dims
    steps, _ = plan_of(space_x, space_y)
    chunks_y = local_y // rows
    chunks = local_x * chunks_y
    boxes = space_x * space_y
    gain_x, gain_y = space_x, space_y
    mx = lax.axis_index("sx")
    my = lax.axis_index("sy")
    me = mx * space_y + my

    barrier = pltpu.get_barrier_semaphore()

    half = space_y // 2
    side, inner = split_index(my, half)
    near_y = side * half
    far_y = (1 - side) * half
    mirror = space_y - 1 - my
    hub = my == 0
    at_edge = inner == (half - 1) * (1 - side)
    low = jnp.logical_and(side == 0, my > 0)
    high = side == 1

    def signal(sem, px, py):
        pl.semaphore_signal(sem, inc=1, device_id=(px, py), device_id_type=MESH)

    @pl.when(side == 0)
    def _():
        for o in range(half):
            signal(barrier, mx, half + lax.rem(inner + o, half))

    @pl.when(low)
    def _():
        signal(barrier, mx, 0)

    @pl.when(high)
    def _():
        signal(barrier, mx, mirror)

        @pl.when(mirror > 0)
        def _():
            signal(barrier, mx, 0)

    @pl.when(hub)
    def _():
        for o in range(1, space_x):
            signal(barrier, lax.rem(mx + o, space_x), 0)

    fetch_mix = pltpu.make_async_copy(mix_hbm, mix_ref, mix_sem)
    fetch_mix.start()
    fetch_deform = pltpu.make_async_copy(deform_hbm, deform_ref, deform_sem)
    fetch_deform.start()

    def piece(k, px, py):
        fx, fy = split_index(k, chunks_y)
        start = pl.multiple_of(py * local_y + fy * rows, 8)
        return coeffs_ref.at[:, 0, px * local_x + fx, 0, pl.ds(start, rows), :]

    def send(k, px, py, lane_sem=None):
        pltpu.make_async_remote_copy(
            src_ref=piece(k, px, py),
            dst_ref=recv.at[k, me],
            send_sem=send_sem,
            recv_sem=recv_sem.at[k if lane_sem is None else lane_sem],
            device_id=(px, py),
            device_id_type=MESH,
        ).start()

    def send_across(k, px, py):
        send(k, px, py, jnp.where(k == chunks - 1, jnp.where(at_edge, chunks + 1, chunks), k))

    def send_line(py):
        def send_one(k, _):
            send_across(k, mx, py)
            return 0

        lax.fori_loop(0, chunks, send_one, 0)

    @pl.when(hub)
    def _():
        pl.semaphore_wait(barrier, space_y - 1 + space_x - 1)
        for o in range(1, space_x):
            signal(plane_sem, lax.rem(mx + o, space_x), 0)
        for o in range(half):
            send_line(half + o)
        pl.semaphore_wait(plane_sem, space_x - 1)
        for o in range(1, space_y):
            signal(go_sem, mx, o)

    @pl.when(low)
    def _():
        pl.semaphore_wait(barrier, 1)
        send_line(mirror)
        pl.semaphore_wait(line_sem, half - 1)
        for o in range(1, half):
            send_line(half + lax.rem(mirror - half + o, half))
        pl.semaphore_wait(go_sem, 1)

    @pl.when(high)
    def _():
        pl.semaphore_wait(barrier, half)
        for o in range(1, half):

            @pl.when(o != mirror)
            def _():
                signal(line_sem, mx, o)

        for o in range(half):
            send_line(half - 1 - o)
        pl.semaphore_wait(go_sem, 1)

    def ahead(px):
        return jnp.where(px < FIRST, 1, 0)

    for c in range(FIRST):
        for o in range(half):

            @pl.when(mx != c)
            def _():
                send(0, c, far_y + lax.rem(inner + o, half))

            @pl.when(jnp.logical_or(mx != c, o > 0))
            def _():
                send(0, c, near_y + lax.rem(inner + o, half))

    def send_chunk(k, _):
        def send_next(send_one, px, py):
            piece_k = k + ahead(px)

            @pl.when(piece_k < chunks)
            def _():
                send_one(piece_k, px, py)

        def send_far(i, _):
            oy, ox = split_index(i, space_x - 1)
            send_next(send_across, jnp.bitwise_xor(mx, space_x - 1 - ox), far_y + lax.rem(inner + oy, half))
            return 0

        def send_near(i, _):
            oy, ox = split_index(i, space_x)
            send_next(send, lax.rem(mx + 1 + ox, space_x), near_y + lax.rem(inner + 1 + oy, half))
            return 0

        lax.fori_loop(0, half * (space_x - 1), send_far, 0)
        lax.fori_loop(0, half * space_x - 1, send_near, 0)
        pltpu.make_async_copy(piece(k, mx, my), recv.at[k, me], recv_sem.at[k]).start()
        return 0

    lax.fori_loop(0, chunks, send_chunk, 0)
    fetch_deform.wait()

    lane = lax.broadcasted_iota(jnp.int32, (1, 128), 1)
    spots = [float(q) for q in cheb_nodes(NODES)]

    def node_of(index):
        node = jnp.full((1, 128), spots[0], jnp.float32)
        for t in range(1, NODES):
            node = jnp.where(index == t, spots[t], node)
        return node

    node_x = node_of(lane // NODES % NODES)
    node_y = node_of(lane % NODES)

    def warped(sx, sy, count):
        box = lax.broadcasted_iota(jnp.int32, (count, 128), 0)
        ax = (box // sy).astype(jnp.float32)
        ay = (box % sy).astype(jnp.float32)
        p1 = (ax + node_x) / sx
        p2 = (ay + node_y) / sy
        y1, y2 = 0.0, 0.0
        for m in range(modes):
            y1 = y1 + deform_ref[0, m] * turns((p1 + p2) * (0.5 * (m + 1)))[1]
            y2 = y2 + deform_ref[1, m] * turns((p1 - p2) * (0.5 * (m + 1)))[1]
        return p1 + y1, p2 + y2

    for along, sx, sy, row in steps[1:]:
        count = max(8, sx * sy)
        y1, y2 = warped(sx, sy, count)
        c, s = turns((y1 * (0.25 * sx)) if along == 0 else (y2 * (0.25 * sy)))
        twid[0, pl.ds(row, count), :] = c
        twid[1, pl.ds(row, count), :] = s

    y1, y2 = warped(space_x, space_y, boxes)
    for fx in range(local_x):
        for child in range(2):
            freq = (mx * local_x + fx).astype(jnp.float32) + (0.25 + 0.5 * child)
            c, s = turns(y1 * (freq * gain_x))
            base1[0, 2 * fx + child] = c
            base1[1, 2 * fx + child] = s
    twid[0, pl.ds(0, boxes), :] = y2

    def base_box(i, _):
        freq = lax.broadcasted_iota(jnp.int32, (local_y, 128), 0) + my * local_y
        warp = twid[0, pl.ds(i, 1), :]
        c, s = turns(warp * ((freq.astype(jnp.float32) + 0.5) * gain_y))
        base2[0, i] = c
        base2[1, i] = s
        return 0

    lax.fori_loop(0, boxes, base_box, 0)

    y1, y2 = warped(1, 1, 8)
    out_x = local_x * space_x
    freq = lax.broadcasted_iota(jnp.int32, (out_x, 128), 0) + mx * out_x
    c, s = turns(y1[0:1] * (freq.astype(jnp.float32) + 0.5))
    last1[0] = c
    last1[1] = s
    for child in range(space_y):
        freq = (lax.broadcasted_iota(jnp.int32, (local_y, 128), 0) + my * local_y) * space_y + child
        c, s = turns(y2[0:1] * (freq.astype(jnp.float32) + 0.5))
        last2[0, child] = c
        last2[1, child] = s

    fetch_mix.wait()

    total, whole_step, subtree, _, finish = butterfly_steps(
        dims, (recv, twid, base1, base2, last1, last2, mix_ref, lhs, state)
    )

    def keep(fx, fy, bx, by, re, im):
        spots = pl.ds(fy * (rows * space_y) + by, rows, stride=space_y)
        out_ref[0, fx * space_x + bx, spots, :] = re
        out_ref[1, fx * space_x + bx, spots, :] = im

    def compute(k, _):
        pltpu.make_async_copy(recv.at[k], recv.at[k], recv_sem.at[k]).wait()
        for number in range(total):
            whole_step(number, k)
        finish(k, keep)
        return 0

    last = chunks - 1
    near = recv.at[last, pl.ds(0, boxes // 2)]
    outer = recv.at[last, pl.ds(0, (half - 1) * space_x)]
    edge = recv.at[last, pl.ds(0, space_x)]
    first, second = max(last - 2, 0), max(last - 1, 0)
    lax.fori_loop(0, first, compute, 0)
    pltpu.make_async_copy(near, near, recv_sem.at[last]).wait()
    partials[-1][...] = subtree(last, near_y, levels - 1)
    lax.fori_loop(first, second, compute, 0)
    if half > 1:
        pltpu.make_async_copy(outer, outer, recv_sem.at[chunks]).wait()
    for level in range(levels - 1):
        line = half + (1 << level) - side * (3 << level)
        partials[level][...] = subtree(last, line, level)
    lax.fori_loop(second, last, compute, 0)
    sent = recv.at[:, pl.ds(0, boxes - 1)]
    pltpu.make_async_copy(sent, sent, send_sem).wait()
    pltpu.make_async_copy(edge, edge, recv_sem.at[chunks + 1]).wait()


def tail_kernel(
    dims,
    done_ref,
    recv,
    twid,
    base1,
    base2,
    last1,
    last2,
    mix_ref,
    *refs,
):
    levels = (dims[1] - 1).bit_length()
    partials = refs[:levels]
    out_hbm, lhs, state, tail, sem = refs[levels:]
    space_x, space_y, local_x, local_y, rows, _ = dims
    chunks_y = local_y // rows
    last = local_x * chunks_y - 1
    start_x, start_y = (local_x - 1) * space_x, (chunks_y - 1) * rows * space_y
    copies = []

    def copy_out(source, target):
        copies.append(pltpu.make_async_copy(source, target, sem.at[len(copies)]))
        copies[-1].start()

    if start_x:
        spot = (slice(None), pl.ds(0, start_x))
        copy_out(done_ref.at[spot], out_hbm.at[spot])
    if start_y:
        spot = (slice(None), pl.ds(start_x, space_x), pl.ds(0, start_y))
        copy_out(done_ref.at[spot], out_hbm.at[spot])

    _, _, _, late_line, finish = butterfly_steps(
        dims, (recv, twid, base1, base2, last1, last2, mix_ref, lhs, state)
    )
    half = space_y // 2
    side = lax.div(lax.axis_index("sy"), half)
    late_line(last, half - side, partials)

    def keep(fx, fy, bx, by, re, im):
        spots = pl.ds(by, rows, stride=space_y)
        tail[0, bx, spots, :] = re
        tail[1, bx, spots, :] = im

    finish(last, keep)
    spot = (slice(None), pl.ds(start_x, space_x), pl.ds(start_y, rows * space_y))
    copy_out(tail, out_hbm.at[spot])
    for copy in copies:
        copy.wait()


def body(coeffs, deform):
    space_x, space_y = lax.axis_size("sx"), lax.axis_size("sy")
    _, _, freq_x, _, freq_y, lanes = coeffs.shape
    local_x, local_y = freq_x // space_x, freq_y // space_y
    rows = ROWS
    chunks = local_x * local_y // rows
    boxes = space_x * space_y
    out_x, out_y = local_x * space_x, local_y * space_y
    right_sides = lanes // NODES**2
    mix = np.stack([mix_matrix(0, right_sides, NODES), mix_matrix(1, right_sides, NODES)])
    high = mix.astype(jnp.bfloat16)
    low = (mix - high.astype(np.float32)).astype(jnp.bfloat16)
    mix = jnp.asarray(np.concatenate([high, low], axis=2))
    _, twid_rows = plan_of(space_x, space_y)
    dims = (space_x, space_y, local_x, local_y, rows, deform.shape[1])
    vmem = pl.BlockSpec(memory_space=pltpu.VMEM)
    state_rows = boxes * 2 * rows
    f32 = jnp.float32
    tables = [
        pltpu.VMEM((chunks, boxes, 2, rows, lanes), f32),
        pltpu.VMEM((2, twid_rows, lanes), f32),
        pltpu.VMEM((2, 2 * local_x, boxes, lanes), f32),
        pltpu.VMEM((2, boxes, local_y, lanes), f32),
        pltpu.VMEM((2, out_x, lanes), f32),
        pltpu.VMEM((2, space_y, local_y, lanes), f32),
        pltpu.VMEM(mix.shape, mix.dtype),
    ]
    tables += [
        pltpu.VMEM((sx * 4 * (rows << number), lanes), f32)
        for number, (along, sx, _, _) in enumerate(plan_of(space_x, space_y)[0])
        if along == 1
    ]
    work = [
        pltpu.VMEM((2, state_rows, 2 * lanes), f32),
        pltpu.VMEM((state_rows, lanes), f32),
    ]
    results = [pltpu.VMEM((2, out_x, out_y, lanes), f32)] + tables
    held = sum(math.prod(ref.shape) * np.dtype(ref.dtype).itemsize for ref in results)
    partial_out = pl.pallas_call(
        functools.partial(kernel, dims),
        out_shape=results,
        in_specs=[pl.BlockSpec(memory_space=pltpu.HBM)] * 3,
        out_specs=[vmem] * len(results),
        scratch_shapes=work
        + [
            pltpu.SemaphoreType.DMA,
            pltpu.SemaphoreType.DMA((chunks + 2,)),
            pltpu.SMEM(deform.shape, f32),
            pltpu.SemaphoreType.DMA,
            pltpu.SemaphoreType.DMA,
            pltpu.SemaphoreType.REGULAR,
            pltpu.SemaphoreType.REGULAR,
            pltpu.SemaphoreType.REGULAR,
        ],
        compiler_params=pltpu.CompilerParams(
            collective_id=0, has_side_effects=True, vmem_limit_bytes=VMEM_ROOM - held - 65536
        ),
        name="butterfly",
    )(deform, mix, coeffs)
    return pl.pallas_call(
        functools.partial(tail_kernel, dims),
        out_shape=jax.ShapeDtypeStruct((2, out_x, out_y, lanes), f32),
        in_specs=[vmem] * len(results),
        out_specs=pl.BlockSpec(memory_space=pl.ANY),
        scratch_shapes=work
        + [
            pltpu.VMEM((2, space_x, rows * space_y, lanes), f32),
            pltpu.SemaphoreType.DMA((3,)),
        ],
        compiler_params=pltpu.CompilerParams(vmem_limit_bytes=VMEM_ROOM // 4),
        name="tail",
    )(*partial_out)


def solution(mesh):
    placed = (P(None, "sx", None, "sy", None, None), P())
    return jax.shard_map(
        body, mesh=mesh, in_specs=placed, out_specs=P(None, "sx", "sy", None), check_vma=False
    )
```

```python
import functools
import math

import jax
import jax.numpy as jnp
import numpy as np
from jax import lax
from jax.experimental import pallas as pl
from jax.experimental.pallas import tpu as pltpu
from jax.sharding import PartitionSpec as P

NODES = 4
FIRST = 2
VMEM_ROOM = 67043328
RHS = 8
ROWS = 8
MESH = pl.DeviceIdType.MESH


def cheb_nodes(count):
    return (1.0 - np.cos(np.pi * (2.0 * np.arange(count) + 1.0) / (2.0 * count))) / 2.0


def lagrange_table(count):
    nodes = cheb_nodes(count)
    table = np.ones((count, 2, count))
    for row in range(count):
        for sibling in range(2):
            spots = (sibling + nodes) / 2.0
            for other in range(count):
                if other != row:
                    table[row, sibling] *= (spots - nodes[other]) / (nodes[row] - nodes[other])
    return table


def mix_matrix(along, right_sides, count):
    table = lagrange_table(count)
    blocks = []
    for sibling in range(2):
        weights = table[:, sibling].T
        eye = np.eye(count)
        inner = np.kron(weights, eye) if along == 0 else np.kron(eye, weights)
        blocks.append(np.kron(np.eye(right_sides), inner))
    return (np.concatenate(blocks, axis=0) * math.sqrt(0.5)).astype(np.float32)


TAYLOR_SIN = [((-1.0) ** k) * (2.0 * math.pi) ** (2 * k + 1) / math.factorial(2 * k + 1) for k in range(8)]
TAYLOR_COS = [((-1.0) ** k) * (2.0 * math.pi) ** (2 * k) / math.factorial(2 * k) for k in range(8)]


def horner(coefs, u):
    acc = coefs[-1] * u + coefs[-2]
    for c in coefs[-3::-1]:
        acc = acc * u + c
    return acc


def turns(t):
    half = jnp.floor(2.0 * t + 0.5)
    rest = t - 0.5 * half
    parity = half - 2.0 * jnp.floor(0.5 * half)
    sign = 1.0 - 2.0 * parity
    u = rest * rest
    return sign * horner(TAYLOR_COS, u), sign * rest * horner(TAYLOR_SIN, u)


def split_index(value, by):
    return lax.div(value, by), lax.rem(value, by)


def plan_of(space_x, space_y):
    steps = []
    sx, sy, row = space_x, space_y, 0
    while sx > 1 or sy > 1:
        if sx > 1:
            steps.append((0, sx, sy, row))
            row += max(8, sx * sy)
            sx //= 2
        if sy > 1:
            steps.append((1, sx, sy, row))
            row += max(8, sx * sy)
            sy //= 2
    return steps, row


def butterfly_steps(dims, refs):
    space_x, space_y, local_x, local_y, rows, _ = dims
    recv, twid, base1, base2, last1, last2, mix_ref, lhs, state = refs
    steps, _ = plan_of(space_x, space_y)
    assert all(step[0] == n % 2 for n, step in enumerate(steps)) and len(steps) % 2 == 1
    chunks_y = local_y // rows
    state_rows = space_x * space_y * 2 * rows

    def place(k):
        fx, fy = split_index(k, chunks_y)
        return fx, fy, pl.ds(pl.multiple_of(fy * rows, 8), rows)

    def rotate_into(slot, pair, sibling, size, re0, im0, re1, im1):
        lines = pl.ds(pair * 4 * size, 4 * size)
        lane = 128 * (sibling or 0)
        lhs[slot, lines, lane : lane + 128] = jnp.concatenate([re0, im0, re1, im1], axis=0)

    def parted(whole):
        high = whole.astype(jnp.bfloat16)
        return high, (whole - high.astype(jnp.float32)).astype(jnp.bfloat16)

    def rotate(number, k, first_y, count_y, alone=False):
        along, sx, sy, row = steps[number]
        fx, _, fy_rows = place(k)
        size = rows << number
        for a1 in range(sx):
            for j in range(count_y):
                table = a1 * sy + first_y + j
                if along == 0:
                    pair, sibling = (a1 // 2) * count_y + j, a1 % 2
                else:
                    pair, sibling = a1 * (count_y + 1 >> 1) + j // 2, None if alone else j % 2
                if number == 0:
                    re, im = recv[k, table, 0], recv[k, table, 1]
                    c, s = base2[0, table, fy_rows, :], base2[1, table, fy_rows, :]
                    re, im = re * c + im * s, im * c - re * s
                    spot = pl.ds(table, 1)
                    c, s = base1[0, 2 * fx, spot, :], base1[1, 2 * fx, spot, :]
                    re0, im0 = re * c + im * s, im * c - re * s
                    c, s = base1[0, 2 * fx + 1, spot, :], base1[1, 2 * fx + 1, spot, :]
                    re1, im1 = re * c + im * s, im * c - re * s
                else:
                    at = (a1 * count_y + j) * 2 * size
                    half = size // 2
                    re = jnp.concatenate(
                        [state[pl.ds(at, half), :], state[pl.ds(at + 2 * half, half), :]], axis=0
                    )
                    im = jnp.concatenate(
                        [state[pl.ds(at + half, half), :], state[pl.ds(at + 3 * half, half), :]], axis=0
                    )
                    spot = pl.ds(row + table, 1)
                    c, s = twid[0, spot, :], twid[1, spot, :]
                    rc, rs, ic, js = re * c, re * s, im * c, im * s
                    re0, im0 = rc - js, ic + rs
                    re1, im1 = rc + js, ic - rs
                rotate_into(number % 2, pair, sibling, size, re0, im0, re1, im1)

    def mixed(number, count):
        slot, along = number % 2, steps[number][0]
        high, low = parted(lhs[slot, 0:count])
        by_high = jnp.dot(high, mix_ref[along], preferred_element_type=jnp.float32)
        by_low = jnp.dot(low, mix_ref[along, :, 0:128], preferred_element_type=jnp.float32)
        return by_high[:, 0:128] + (by_high[:, 128:256] + by_low)

    def mixed_alone(number, sibling, count):
        slot, along = number % 2, steps[number][0]
        deep = mix_ref[along, pl.ds(pl.multiple_of(sibling * 128, 128), 128), :]
        both = jnp.concatenate([deep, deep], axis=0)
        pair = jnp.concatenate(parted(lhs[slot, 0:count, 0:128]), axis=1)
        by = jnp.dot(pair, both, preferred_element_type=jnp.float32)
        return by[:, 0:128] + by[:, 128:256]

    def whole_step(number, k):
        rotate(number, k, 0, steps[number][2])
        state[...] = mixed(number, state_rows)

    def lone_step(number, k, line):
        box = lax.div(line, 1 << number // 2)
        sibling = lax.rem(box, 2)
        rotate(number, k, box, 1, alone=True)
        return mixed_alone(number, sibling, steps[number][1] * 4 * (rows << number))

    def subtree(k, line, level):
        for number in range(2 * level + 1):
            _, sx, _, _ = steps[number]
            count_y = (1 << level) >> (number // 2)
            first_y = lax.div(line, 1 << number // 2)
            rotate(number, k, first_y, count_y)
            count = sx * count_y * 2 * (rows << number)
            state[0:count] = mixed(number, count)
        return lone_step(2 * level + 1, k, line)

    def late_line(k, line, partials):
        for number in range(len(steps) - 1):
            _, sx, _, _ = steps[number]
            if number % 2:
                partial = partials[number // 2]
                state[0 : partial.shape[0]] = partial[...] + lone_step(number, k, line)
            else:
                rotate(number, k, lax.div(line, 1 << number // 2), 1)
                count = sx * 2 * (rows << number)
                state[0:count] = mixed(number, count)
        whole_step(len(steps) - 1, k)

    def finish(k, store):
        fx, fy, fy_rows = place(k)
        total = len(steps)
        ends = []
        for code in range(1 << total):
            bits = [(code >> n) & 1 for n in range(total)]
            at = 0
            for n in range(total - 1):
                at += bits[n] * rows * (1 << n)
            half = rows * (1 << (total - 1))
            at += bits[total - 1] * 2 * half
            bx, by = 0, 0
            for n, (along, _, _, _) in enumerate(steps):
                if along == 0:
                    bx = 2 * bx + bits[n]
                else:
                    by = 2 * by + bits[n]
            ends.append((bx, by, at, at + half))
        for bx, by, at_re, at_im in sorted(ends):
            re = state[pl.ds(at_re, rows), :]
            im = state[pl.ds(at_im, rows), :]
            first = fx * space_x + bx
            c1, s1 = last1[0, pl.ds(first, 1), :], last1[1, pl.ds(first, 1), :]
            c2, s2 = last2[0, by, fy_rows, :], last2[1, by, fy_rows, :]
            c = c1 * c2 - s1 * s2
            s = s1 * c2 + c1 * s2
            store(fx, fy, bx, by, re * c - im * s, im * c + re * s)

    return len(steps), whole_step, subtree, late_line, finish


def kernel(
    dims,
    deform_hbm,
    mix_hbm,
    coeffs_ref,
    out_ref,
    recv,
    twid,
    base1,
    base2,
    last1,
    last2,
    mix_ref,
    *refs,
):
    levels = (dims[1] - 1).bit_length()
    partials = refs[:levels]
    (
        lhs,
        state,
        send_sem,
        recv_sem,
        deform_ref,
        deform_sem,
        mix_sem,
        plane_sem,
        go_sem,
        line_sem,
    ) = refs[levels:]
    space_x, space_y, local_x, local_y, rows, modes = dims
    steps, _ = plan_of(space_x, space_y)
    chunks_y = local_y // rows
    chunks = local_x * chunks_y
    boxes = space_x * space_y
    gain_x, gain_y = space_x, space_y
    mx = lax.axis_index("sx")
    my = lax.axis_index("sy")
    me = mx * space_y + my

    barrier = pltpu.get_barrier_semaphore()

    half = space_y // 2
    side, inner = split_index(my, half)
    near_y = side * half
    far_y = (1 - side) * half
    mirror = space_y - 1 - my
    hub = my == 0
    at_edge = inner == (half - 1) * (1 - side)
    low = jnp.logical_and(side == 0, my > 0)
    high = side == 1

    def signal(sem, px, py):
        pl.semaphore_signal(sem, inc=1, device_id=(px, py), device_id_type=MESH)

    @pl.when(side == 0)
    def _():
        for o in range(half):
            signal(barrier, mx, half + lax.rem(inner + o, half))

    @pl.when(low)
    def _():
        signal(barrier, mx, 0)

    @pl.when(high)
    def _():
        signal(barrier, mx, mirror)

        @pl.when(mirror > 0)
        def _():
            signal(barrier, mx, 0)

    @pl.when(hub)
    def _():
        for o in range(1, space_x):
            signal(barrier, lax.rem(mx + o, space_x), 0)

    fetch_mix = pltpu.make_async_copy(mix_hbm, mix_ref, mix_sem)
    fetch_mix.start()
    fetch_deform = pltpu.make_async_copy(deform_hbm, deform_ref, deform_sem)
    fetch_deform.start()

    def piece(k, px, py):
        fx, fy = split_index(k, chunks_y)
        start = pl.multiple_of(py * local_y + fy * rows, 8)
        return coeffs_ref.at[:, 0, px * local_x + fx, 0, pl.ds(start, rows), :]

    def send(k, px, py, lane_sem=None):
        pltpu.make_async_remote_copy(
            src_ref=piece(k, px, py),
            dst_ref=recv.at[k, me],
            send_sem=send_sem,
            recv_sem=recv_sem.at[k if lane_sem is None else lane_sem],
            device_id=(px, py),
            device_id_type=MESH,
        ).start()

    def send_across(k, px, py):
        send(k, px, py, jnp.where(k == chunks - 1, jnp.where(at_edge, chunks + 1, chunks), k))

    def send_line(py):
        def send_one(k, _):
            send_across(k, mx, py)
            return 0

        lax.fori_loop(0, chunks, send_one, 0)

    @pl.when(hub)
    def _():
        pl.semaphore_wait(barrier, space_y - 1 + space_x - 1)
        for o in range(1, space_x):
            signal(plane_sem, lax.rem(mx + o, space_x), 0)
        for o in range(half):
            send_line(half + o)
        pl.semaphore_wait(plane_sem, space_x - 1)
        for o in range(1, space_y):
            signal(go_sem, mx, o)

    @pl.when(low)
    def _():
        pl.semaphore_wait(barrier, 1)
        send_line(mirror)
        pl.semaphore_wait(line_sem, half - 1)
        for o in range(1, half):
            send_line(half + lax.rem(mirror - half + o, half))
        pl.semaphore_wait(go_sem, 1)

    @pl.when(high)
    def _():
        pl.semaphore_wait(barrier, half)
        for o in range(1, half):

            @pl.when(o != mirror)
            def _():
                signal(line_sem, mx, o)

        for o in range(half):
            send_line(half - 1 - o)
        pl.semaphore_wait(go_sem, 1)

    def ahead(px, py):
        return jnp.where(px < FIRST, jnp.where(py == 0, 2, 1), 0)

    for c in range(FIRST):
        for o in range(half):

            @pl.when(mx != c)
            def _():
                send(0, c, far_y + lax.rem(inner + o, half))

            @pl.when(jnp.logical_or(mx != c, o > 0))
            def _():
                send(0, c, near_y + lax.rem(inner + o, half))

    for c in range(FIRST):

        @pl.when(jnp.logical_and(high, mx != c))
        def _():
            send_across(1, c, 0)

        @pl.when(jnp.logical_and(side == 0, jnp.logical_or(mx != c, low)))
        def _():
            send(1, c, 0)

    def send_chunk(k, _):
        def send_next(send_one, px, py):
            piece_k = k + ahead(px, py)

            @pl.when(piece_k < chunks)
            def _():
                send_one(piece_k, px, py)

        def send_far(i, _):
            oy, ox = split_index(i, space_x - 1)
            send_next(send_across, jnp.bitwise_xor(mx, space_x - 1 - ox), far_y + lax.rem(inner + oy, half))
            return 0

        def send_near(i, _):
            oy, ox = split_index(i, space_x)
            send_next(send, lax.rem(mx + 1 + ox, space_x), near_y + lax.rem(inner + 1 + oy, half))
            return 0

        lax.fori_loop(0, half * (space_x - 1), send_far, 0)
        lax.fori_loop(0, half * space_x - 1, send_near, 0)
        pltpu.make_async_copy(piece(k, mx, my), recv.at[k, me], recv_sem.at[k]).start()
        return 0

    lax.fori_loop(0, chunks, send_chunk, 0)
    fetch_deform.wait()

    lane = lax.broadcasted_iota(jnp.int32, (1, 128), 1)
    spots = [float(q) for q in cheb_nodes(NODES)]

    def node_of(index):
        node = jnp.full((1, 128), spots[0], jnp.float32)
        for t in range(1, NODES):
            node = jnp.where(index == t, spots[t], node)
        return node

    node_x = node_of(lane // NODES % NODES)
    node_y = node_of(lane % NODES)

    def warped(sx, sy, count):
        box = lax.broadcasted_iota(jnp.int32, (count, 128), 0)
        ax = (box // sy).astype(jnp.float32)
        ay = (box % sy).astype(jnp.float32)
        p1 = (ax + node_x) / sx
        p2 = (ay + node_y) / sy
        y1, y2 = 0.0, 0.0
        for m in range(modes):
            y1 = y1 + deform_ref[0, m] * turns((p1 + p2) * (0.5 * (m + 1)))[1]
            y2 = y2 + deform_ref[1, m] * turns((p1 - p2) * (0.5 * (m + 1)))[1]
        return p1 + y1, p2 + y2

    for along, sx, sy, row in steps[1:]:
        count = max(8, sx * sy)
        y1, y2 = warped(sx, sy, count)
        c, s = turns((y1 * (0.25 * sx)) if along == 0 else (y2 * (0.25 * sy)))
        twid[0, pl.ds(row, count), :] = c
        twid[1, pl.ds(row, count), :] = s

    y1, y2 = warped(space_x, space_y, boxes)
    for fx in range(local_x):
        for child in range(2):
            freq = (mx * local_x + fx).astype(jnp.float32) + (0.25 + 0.5 * child)
            c, s = turns(y1 * (freq * gain_x))
            base1[0, 2 * fx + child] = c
            base1[1, 2 * fx + child] = s
    twid[0, pl.ds(0, boxes), :] = y2

    def base_box(i, _):
        freq = lax.broadcasted_iota(jnp.int32, (local_y, 128), 0) + my * local_y
        warp = twid[0, pl.ds(i, 1), :]
        c, s = turns(warp * ((freq.astype(jnp.float32) + 0.5) * gain_y))
        base2[0, i] = c
        base2[1, i] = s
        return 0

    lax.fori_loop(0, boxes, base_box, 0)

    y1, y2 = warped(1, 1, 8)
    out_x = local_x * space_x
    freq = lax.broadcasted_iota(jnp.int32, (out_x, 128), 0) + mx * out_x
    c, s = turns(y1[0:1] * (freq.astype(jnp.float32) + 0.5))
    last1[0] = c
    last1[1] = s
    for child in range(space_y):
        freq = (lax.broadcasted_iota(jnp.int32, (local_y, 128), 0) + my * local_y) * space_y + child
        c, s = turns(y2[0:1] * (freq.astype(jnp.float32) + 0.5))
        last2[0, child] = c
        last2[1, child] = s

    fetch_mix.wait()

    total, whole_step, subtree, _, finish = butterfly_steps(
        dims, (recv, twid, base1, base2, last1, last2, mix_ref, lhs, state)
    )

    def keep(fx, fy, bx, by, re, im):
        spots = pl.ds(fy * (rows * space_y) + by, rows, stride=space_y)
        out_ref[0, fx * space_x + bx, spots, :] = re
        out_ref[1, fx * space_x + bx, spots, :] = im

    def compute(k, _):
        pltpu.make_async_copy(recv.at[k], recv.at[k], recv_sem.at[k]).wait()
        for number in range(total):
            whole_step(number, k)
        finish(k, keep)
        return 0

    last = chunks - 1
    near = recv.at[last, pl.ds(0, boxes // 2)]
    outer = recv.at[last, pl.ds(0, (half - 1) * space_x)]
    edge = recv.at[last, pl.ds(0, space_x)]
    first, second = max(last - 2, 0), max(last - 1, 0)
    lax.fori_loop(0, first, compute, 0)
    pltpu.make_async_copy(near, near, recv_sem.at[last]).wait()
    partials[-1][...] = subtree(last, near_y, levels - 1)
    lax.fori_loop(first, second, compute, 0)
    if half > 1:
        pltpu.make_async_copy(outer, outer, recv_sem.at[chunks]).wait()
    for level in range(levels - 1):
        line = half + (1 << level) - side * (3 << level)
        partials[level][...] = subtree(last, line, level)
    lax.fori_loop(second, last, compute, 0)
    sent = recv.at[:, pl.ds(0, boxes - 1)]
    pltpu.make_async_copy(sent, sent, send_sem).wait()
    pltpu.make_async_copy(edge, edge, recv_sem.at[chunks + 1]).wait()


def tail_kernel(
    dims,
    done_ref,
    recv,
    twid,
    base1,
    base2,
    last1,
    last2,
    mix_ref,
    *refs,
):
    levels = (dims[1] - 1).bit_length()
    partials = refs[:levels]
    out_hbm, lhs, state, tail, sem = refs[levels:]
    space_x, space_y, local_x, local_y, rows, _ = dims
    chunks_y = local_y // rows
    last = local_x * chunks_y - 1
    start_x, start_y = (local_x - 1) * space_x, (chunks_y - 1) * rows * space_y
    copies = []

    def copy_out(source, target):
        copies.append(pltpu.make_async_copy(source, target, sem.at[len(copies)]))
        copies[-1].start()

    if start_x:
        spot = (slice(None), pl.ds(0, start_x))
        copy_out(done_ref.at[spot], out_hbm.at[spot])
    if start_y:
        spot = (slice(None), pl.ds(start_x, space_x), pl.ds(0, start_y))
        copy_out(done_ref.at[spot], out_hbm.at[spot])

    _, _, _, late_line, finish = butterfly_steps(
        dims, (recv, twid, base1, base2, last1, last2, mix_ref, lhs, state)
    )
    half = space_y // 2
    side = lax.div(lax.axis_index("sy"), half)
    late_line(last, half - side, partials)

    def keep(fx, fy, bx, by, re, im):
        spots = pl.ds(by, rows, stride=space_y)
        tail[0, bx, spots, :] = re
        tail[1, bx, spots, :] = im

    finish(last, keep)
    spot = (slice(None), pl.ds(start_x, space_x), pl.ds(start_y, rows * space_y))
    copy_out(tail, out_hbm.at[spot])
    for copy in copies:
        copy.wait()


def body(coeffs, deform):
    space_x, space_y = lax.axis_size("sx"), lax.axis_size("sy")
    _, _, freq_x, _, freq_y, lanes = coeffs.shape
    local_x, local_y = freq_x // space_x, freq_y // space_y
    rows = ROWS
    chunks = local_x * local_y // rows
    boxes = space_x * space_y
    out_x, out_y = local_x * space_x, local_y * space_y
    right_sides = lanes // NODES**2
    mix = np.stack([mix_matrix(0, right_sides, NODES), mix_matrix(1, right_sides, NODES)])
    high = mix.astype(jnp.bfloat16)
    low = (mix - high.astype(np.float32)).astype(jnp.bfloat16)
    mix = jnp.asarray(np.concatenate([high, low], axis=2))
    _, twid_rows = plan_of(space_x, space_y)
    dims = (space_x, space_y, local_x, local_y, rows, deform.shape[1])
    vmem = pl.BlockSpec(memory_space=pltpu.VMEM)
    state_rows = boxes * 2 * rows
    f32 = jnp.float32
    tables = [
        pltpu.VMEM((chunks, boxes, 2, rows, lanes), f32),
        pltpu.VMEM((2, twid_rows, lanes), f32),
        pltpu.VMEM((2, 2 * local_x, boxes, lanes), f32),
        pltpu.VMEM((2, boxes, local_y, lanes), f32),
        pltpu.VMEM((2, out_x, lanes), f32),
        pltpu.VMEM((2, space_y, local_y, lanes), f32),
        pltpu.VMEM(mix.shape, mix.dtype),
    ]
    tables += [
        pltpu.VMEM((sx * 4 * (rows << number), lanes), f32)
        for number, (along, sx, _, _) in enumerate(plan_of(space_x, space_y)[0])
        if along == 1
    ]
    work = [
        pltpu.VMEM((2, state_rows, 2 * lanes), f32),
        pltpu.VMEM((state_rows, lanes), f32),
    ]
    results = [pltpu.VMEM((2, out_x, out_y, lanes), f32)] + tables
    held = sum(math.prod(ref.shape) * np.dtype(ref.dtype).itemsize for ref in results)
    partial_out = pl.pallas_call(
        functools.partial(kernel, dims),
        out_shape=results,
        in_specs=[pl.BlockSpec(memory_space=pltpu.HBM)] * 3,
        out_specs=[vmem] * len(results),
        scratch_shapes=work
        + [
            pltpu.SemaphoreType.DMA,
            pltpu.SemaphoreType.DMA((chunks + 2,)),
            pltpu.SMEM(deform.shape, f32),
            pltpu.SemaphoreType.DMA,
            pltpu.SemaphoreType.DMA,
            pltpu.SemaphoreType.REGULAR,
            pltpu.SemaphoreType.REGULAR,
            pltpu.SemaphoreType.REGULAR,
        ],
        compiler_params=pltpu.CompilerParams(
            collective_id=0, has_side_effects=True, vmem_limit_bytes=VMEM_ROOM - held - 65536
        ),
        name="butterfly",
    )(deform, mix, coeffs)
    return pl.pallas_call(
        functools.partial(tail_kernel, dims),
        out_shape=jax.ShapeDtypeStruct((2, out_x, out_y, lanes), f32),
        in_specs=[vmem] * len(results),
        out_specs=pl.BlockSpec(memory_space=pl.ANY),
        scratch_shapes=work
        + [
            pltpu.VMEM((2, space_x, rows * space_y, lanes), f32),
            pltpu.SemaphoreType.DMA((3,)),
        ],
        compiler_params=pltpu.CompilerParams(vmem_limit_bytes=VMEM_ROOM // 4),
        name="tail",
    )(*partial_out)


def solution(mesh):
    placed = (P(None, "sx", None, "sy", None, None), P())
    return jax.shard_map(
        body, mesh=mesh, in_specs=placed, out_specs=P(None, "sx", "sy", None), check_vma=False
    )
```
